128 devices in a mesh: line: 8 (over y, core), tile: 16 (over x, z).
Axes of the slice: x: 4, y: 4, z: 4, core: 2. Of those that a mesh axis runs over, the one named last changes fastest.
Arguments:
- traces: bfloat16 [16, 4096, 128], P('tile', 'line'), may hold values from -6 to 6
- codes: int32 [16, 64], P('tile'), may hold values from 0 to 255
- routes: int32 [8, 256], P('line', 'tile'), may hold values from 0 to 15, as said below
- beam_matrix: bfloat16 [8, 16, 2, 4096, 1024], P('line', 'tile'), may hold values from -0.046875 to 0.046875
- dip_filter: float32 [5, 5], replicated, may hold values from -1 to 1
Outputs:
- migrated: float32 [2, 64, 128, 128], P(None, 'line', 'tile')
The draws below stay inside these ranges and needn't reach their ends.
Inputs may be any that keep to these rules, and one draw needn't show every extreme that they name: `routes`: entry [l, f * 16 + b] is the depth tile that block b of frequency f on line l goes to. Among the 16 entries of one device no tile appears more than 4 times, and in every line some device names one tile exactly 4 times. Among the entries of one line no tile appears more than 32 times, and in every line one tile appears exactly 32 times.
All inputs are finite; a program needn't handle non-finite values.
Results may differ from the reference program's by a relative error of at most 0.004.
Values may be sent and summed in bfloat16 or wider, within the bound.
No kernel may reach another device: no remote copies, remote signals or barrier semaphores. Data moves between devices by JAX's collectives and lax.ppermute only.
A program may use at most 64 MiB of HBM per device.

```python
import jax
import jax.numpy as jnp
from jax import lax

S = 64
P_SIZE = 256
WIN = 128
BR = 128
TZ = 8
TX = 128
MAXB = 32
SEND_MOST = 4
F = 16
NB = 16
TRACES = 4096
NZ = 128
N_LINE = 8
N_TILE = 16


def draw_routes(key, part):
    per_owner = MAXB // N_TILE
    spread = N_TILE - 2

    def one_line(line_key):
        key_hot, key_warm, key_rest = jax.random.split(line_key, 3)
        hot_tile = jax.random.randint(key_hot, (), 0, N_TILE)
        offset_warm = jax.random.randint(key_warm, (), 0, N_TILE - 1)
        senders = jnp.arange(N_TILE)
        warm_tiles = (hot_tile + 1 + (senders + offset_warm) % (N_TILE - 1)) % N_TILE

        def one_sender(sender_key, warm_tile):
            key_order, key_blocks = jax.random.split(sender_key)
            shuffled = jax.random.permutation(key_order, N_TILE)
            reserved = ((shuffled == hot_tile) | (shuffled == warm_tile)).astype(jnp.int32)
            spare_tiles = shuffled[jnp.argsort(reserved, stable=True)]
            places = jnp.arange(NB)
            extra_tiles = spare_tiles[jnp.maximum(places - per_owner - SEND_MOST, 0) % spread]
            owners = jnp.where(places < per_owner, hot_tile, jnp.where(places < per_owner + SEND_MOST, warm_tile, extra_tiles))
            return owners[jax.random.permutation(key_blocks, NB)]
        return jax.vmap(one_sender)(jax.random.split(key_rest, N_TILE), warm_tiles).reshape(-1)
    return jax.vmap(one_line)(jax.random.split(key, N_LINE)).astype(jnp.int32)


def plant(drawn, rng, least, high):
    longest = drawn.shape.index(max(drawn.shape))
    spots = []
    for shift in (0, 1):
        where = [jax.random.randint(jax.random.fold_in(rng, axis), (), 0, length) for axis, length in enumerate(drawn.shape)]
        where[longest] = (where[longest] + shift) % drawn.shape[longest]
        spots.append(tuple(where))
    return drawn.at[spots[0]].set(least).at[spots[1]].set(high)


def level_of(key, shape, shards, least, largest):
    loudness = 1.0
    for axis_at, parts in shards:
        heights = jax.random.uniform(jax.random.fold_in(jax.random.fold_in(key, 6), axis_at), (parts,), jnp.float32, least / len(shards), largest / len(shards))
        loudness = loudness * jnp.repeat(jnp.exp(heights), shape[axis_at] // parts).reshape((-1,) + (1,) * (len(shape) - 1 - axis_at))
    return loudness


def bell_draw(rng, dims, deviation, limit, pieces=(), held_as=jnp.bfloat16):
    level = level_of(rng, dims, pieces, -0.22, 0.18) if pieces else 1.0
    entries = jax.random.normal(rng, dims, jnp.float32) * deviation * level
    return jnp.minimum(jnp.maximum(entries, -limit), limit).astype(held_as)


def setup_inputs(seed: int = 0) -> dict:
    key_of = jax.random.split(jax.random.key(seed), 6)
    traces = bell_draw(key_of[0], (F, TRACES, 2 * S), 1.0, 6.0, ((0, 16), (1, 8)))
    codes = plant(jax.random.randint(key_of[1], (F, S), 0, 256), jax.random.fold_in(key_of[1], 1), 0, 255).astype(jnp.int32)
    routes = draw_routes(jax.random.fold_in(key_of[5], 71), 0)
    beam_matrix = bell_draw(key_of[3], (N_LINE, N_TILE, 2, MAXB * BR, TZ * TX), (4 * MAXB * BR) ** -0.5, 0.046875, ((0, 8), (1, 16)))
    dip_filter = bell_draw(key_of[4], (5, 5), 0.2, 1.0, (), jnp.float32)
    return dict(traces=traces, codes=codes, routes=routes, beam_matrix=beam_matrix, dip_filter=dip_filter)


def slant_table(frequency, freq_count):
    slopes = jnp.arange(P_SIZE, dtype=jnp.float32) - P_SIZE / 2
    offsets = jnp.arange(WIN, dtype=jnp.float32) - (WIN - 1) / 2
    factor = 2.0 + frequency.astype(jnp.float32) / freq_count
    phase_angle = jnp.pi * factor * slopes[:, None] * offsets[None, :] / WIN
    taper_row = jnp.exp(-0.5 * (offsets / (0.4 * WIN)) ** 2)
    taper_row = taper_row / jnp.sqrt(jnp.sum(taper_row * taper_row))
    return jnp.concatenate([taper_row * jnp.cos(phase_angle), -taper_row * jnp.sin(phase_angle)], 0).astype(jnp.bfloat16)

def rotate(stacked, code_row):
    real_part = stacked[..., :P_SIZE, :S] - stacked[..., P_SIZE:, S:]
    imag_part = stacked[..., :P_SIZE, S:] + stacked[..., P_SIZE:, :S]
    code_angle = 2.0 * jnp.pi * code_row.astype(jnp.float32) / 256.0
    cosine = jnp.cos(code_angle)
    sine_part = jnp.sin(code_angle)
    return jnp.concatenate([real_part * cosine + imag_part * sine_part, imag_part * cosine - real_part * sine_part], -1).astype(jnp.bfloat16)

def dip_apply(padded, dip_filter):
    depth_rows = padded.shape[2] - 4
    widened = jnp.pad(padded, ((0, 0), (0, 0), (0, 0), (2, 2)))
    result = jnp.zeros(padded.shape[:2] + (depth_rows, TX), jnp.float32)
    for down_step in range(5):
        for side_step in range(5):
            result = result + dip_filter[down_step, side_step] * widened[:, :, down_step:down_step + depth_rows, side_step:side_step + TX]
    return result

def reference(traces, codes, routes, beam_matrix, dip_filter):
    tables = jax.vmap(lambda frequency: slant_table(frequency, F))(jnp.arange(F))
    half_win = WIN // 2
    extended = jnp.concatenate([traces, jnp.zeros((F, half_win, 2 * S), traces.dtype)], 1)
    halves = extended.reshape(F, -1, half_win, 2 * S)
    windows = jnp.concatenate([halves[:, :-1], halves[:, 1:]], 2)
    stacked = jnp.einsum('fpj,fmjc->fmpc', tables.astype(jnp.float32), windows.astype(jnp.float32), precision=lax.Precision.HIGHEST)
    beam_rows = rotate(stacked, codes[:, None, None, :])
    blocks = beam_rows.reshape(F, N_LINE, NB, BR * 2 * S)
    per_line = jnp.transpose(blocks, (1, 0, 2, 3)).reshape(N_LINE, F * NB, BR * 2 * S)

    def tile_image(tile_id):

        def add_line(total, line_id):
            is_mine = (routes[line_id] == tile_id).astype(jnp.int32)
            slot_ids = jnp.where(is_mine > 0, jnp.cumsum(is_mine) - 1, MAXB).astype(jnp.int32)
            compact = jnp.zeros((MAXB, BR * 2 * S), jnp.bfloat16).at[slot_ids].set(per_line[line_id], mode='drop')
            slot_rows = compact.reshape(MAXB * BR, 2 * S)
            matrices = beam_matrix[line_id, tile_id]
            with_real = jnp.dot(slot_rows.T, matrices[0], preferred_element_type=jnp.float32)
            with_imag = jnp.dot(slot_rows.T, matrices[1], preferred_element_type=jnp.float32)
            image_re = with_real[:S] - with_imag[S:]
            image_im = with_real[S:] + with_imag[:S]
            return (total + jnp.stack([image_re, image_im]), None)
        total, ignored = lax.scan(add_line, jnp.zeros((2, S, TZ * TX), jnp.float32), jnp.arange(N_LINE))
        return total
    images = lax.map(tile_image, jnp.arange(N_TILE))
    image_all = images.reshape(N_TILE, 2, S, TZ, TX).transpose(1, 2, 0, 3, 4).reshape(2, S, NZ, TX)
    padded = jnp.pad(image_all, ((0, 0), (0, 0), (2, 2), (0, 0)))
    return dip_apply(padded, dip_filter)
```

```python
import jax
import jax.numpy as jnp
from jax import lax
from jax.experimental import pallas as pl
from jax.experimental.pallas import tpu as pltpu
from jax.sharding import PartitionSpec as P

S = 64
P_SIZE = 256
WIN = 128
BR = 128
TZ = 8
TX = 128
MAXB = 32
NB = 16
HALF = WIN // 2
LOCAL = 512
AUX = LOCAL + HALF
ROWS = AUX + 16
SIDE = 4
RING = (0, 1, 3, 2)
BOTH = ("line", "tile")
N_LINE = 8
N_TILE = 16
CHUNK = 256
CHUNKS = MAXB * BR // CHUNK


def hops(offset, x_first):
    pairs = []
    for line in range(N_LINE):
        along_x = x_first == (line % 2 == 0)
        for x in range(SIDE):
            for z in range(SIDE):
                to_x, to_z = ((x + offset) % SIDE, z) if along_x else (x, (z + offset) % SIDE)
                pairs.append((line * N_TILE + x * SIDE + z, line * N_TILE + to_x * SIDE + to_z))
    return pairs


def table_kernel(out_ref):
    rows = lax.broadcasted_iota(jnp.int32, (WIN, P_SIZE), 0)
    cols = lax.broadcasted_iota(jnp.int32, (WIN, P_SIZE), 1)
    turns = (cols - P_SIZE // 2) * (2 * rows - (WIN - 1))
    unit = 2.0 * jnp.pi / 8192.0
    step = (((turns + 4096) & 8191) - 4096).astype(jnp.float32) * unit
    base = (((32 * turns + 4096) & 8191) - 4096).astype(jnp.float32) * unit
    offsets = lax.broadcasted_iota(jnp.int32, (WIN, 1), 0).astype(jnp.float32) - (WIN - 1) / 2
    taper = jnp.exp(-0.5 * (offsets / (0.4 * WIN)) ** 2)
    taper = taper / jnp.sqrt(jnp.sum(taper * taper, axis=0, keepdims=True))
    step_c, step_s = jnp.cos(step), jnp.sin(step)
    now_c, now_s = taper * jnp.cos(base), -taper * jnp.sin(base)
    for f in range(N_TILE):
        for q in range(2):
            half = slice(q * BR, (q + 1) * BR)
            out_ref[2 * f + q, :, :BR] = now_c[:, half].astype(jnp.bfloat16)
            out_ref[2 * f + q, :, BR:] = now_s[:, half].astype(jnp.bfloat16)
        now_c, now_s = now_c * step_c + now_s * step_s, now_s * step_c - now_c * step_s


def slant_tables():
    return pl.pallas_call(
        table_kernel,
        out_shape=jax.ShapeDtypeStruct((2 * N_TILE, WIN, 2 * BR), jnp.bfloat16),
        out_specs=pl.BlockSpec(memory_space=pltpu.VMEM),
        compiler_params=pltpu.CompilerParams(vmem_limit_bytes=16 * 2**20),
        name="slant_tables",
    )()


def place_of(offset):
    return jnp.where(offset == 2, 3, jnp.where(offset == 3, 2, offset))


def image_kernel(
    where_ref, own_ref, one_ref, three_ref, two_ref, table_ref, matrix_ref, out_ref,
    gathered, cos_ref, sin_ref, slots_re, slots_im, total, list_v, list_s, matrix_v, part_sem, matrix_sem, list_sem,
):
    tile, x, z, parity = where_ref[0], where_ref[1], where_ref[2], where_ref[3]
    parts = (own_ref, one_ref, three_ref, two_ref)
    part_copies = [
        pltpu.make_async_copy(part, gathered.at[pl.ds(SIDE * j, SIDE)], part_sem.at[j]) for j, part in enumerate(parts)
    ]
    for copy in part_copies:
        copy.start()

    def matrix_copy(c):
        rows = pl.ds(pl.multiple_of(c * CHUNK, CHUNK), CHUNK)
        return pltpu.make_async_copy(matrix_ref.at[0, 0, :, rows, :], matrix_v.at[c], matrix_sem.at[c])

    for c in range(CHUNKS):
        matrix_copy(c).start()
    for copy in part_copies:
        copy.wait()

    def place(f):
        dx, dz = (x - f // SIDE) & 3, (z - f % SIDE) & 3
        px, pz = place_of(dx), place_of(dz)
        return jnp.where(parity == 0, px * SIDE + pz, pz * SIDE + px)

    route_rows = [gathered[place(jnp.int32(f)), AUX : AUX + 8, :].astype(jnp.float32) for f in range(N_TILE)]
    routes = jnp.concatenate([row[0:1] for row in route_rows], 0)
    codes = jnp.concatenate([row[1:2] for row in route_rows], 0)
    lane = lax.broadcasted_iota(jnp.int32, (N_TILE, WIN), 1)
    mine = jnp.where((lane < NB) & (routes == tile.astype(jnp.float32)), 1.0, 0.0)
    lane_r = lax.broadcasted_iota(jnp.int32, (WIN, WIN), 0)
    lane_c = lax.broadcasted_iota(jnp.int32, (WIN, WIN), 1)
    before_b = jnp.dot(mine, jnp.where(lane_r < lane_c, 1.0, 0.0), preferred_element_type=jnp.float32)
    counts = jnp.dot(mine, jnp.ones((WIN, WIN), jnp.float32), preferred_element_type=jnp.float32)
    f_r = lax.broadcasted_iota(jnp.int32, (N_TILE, N_TILE), 0)
    f_c = lax.broadcasted_iota(jnp.int32, (N_TILE, N_TILE), 1)
    before_f = jnp.dot(jnp.where(f_c < f_r, 1.0, 0.0), counts, preferred_element_type=jnp.float32)
    rank = jnp.where(mine > 0.0, before_b + before_f, -1.0)
    slot_row = lax.broadcasted_iota(jnp.int32, (MAXB, WIN), 0).astype(jnp.float32)
    lane_wide = lax.broadcasted_iota(jnp.int32, (MAXB, WIN), 1)
    found = jnp.zeros((MAXB, WIN), jnp.float32)
    for f in range(N_TILE):
        hit = rank[f : f + 1] == slot_row
        found = found + jnp.where(hit, (lane_wide + NB * f).astype(jnp.float32), 0.0)
    which = jnp.sum(found, 1, keepdims=True)
    total_count = jnp.sum(counts[:, 0:1], 0, keepdims=True)
    listed = jnp.concatenate([jnp.broadcast_to(which, (MAXB, WIN)), jnp.broadcast_to(total_count, (8, WIN))], 0)
    list_v[...] = listed.astype(jnp.int32)
    list_copy = pltpu.make_async_copy(list_v, list_s, list_sem)
    list_copy.start()

    code_cols = jnp.concatenate([codes, jnp.zeros((WIN - N_TILE, WIN), jnp.float32)], 0).T[:S]
    angles = code_cols * (2.0 * jnp.pi / 256.0)
    cosines, sines = jnp.cos(angles), jnp.sin(angles)
    for f in range(N_TILE):
        cos_ref[f] = jnp.broadcast_to(cosines[:, f : f + 1], (S, BR))
        sin_ref[f] = jnp.broadcast_to(sines[:, f : f + 1], (S, BR))
    list_copy.wait()
    count = list_s[MAXB, 0]

    def interleave(real, imag):
        pieces = []
        for d in range(N_LINE):
            pieces += [real[8 * d : 8 * d + 8], imag[8 * d : 8 * d + 8]]
        return jnp.concatenate(pieces, 0)

    def one_slot(n):
        block = list_s[n, 0]
        f, b = block // NB, block % NB
        rows = pl.ds(pl.multiple_of((b // 2) * HALF, HALF), WIN)
        window = gathered[place(f), rows, :]
        stacked = lax.dot_general(
            window, table_ref[2 * f + b % 2], (((0,), (0,)), ((), ())), preferred_element_type=jnp.float32
        )
        real = stacked[:S, :BR] - stacked[S:, BR:]
        imag = stacked[S:, :BR] + stacked[:S, BR:]
        cosine, sine = cos_ref[f], sin_ref[f]
        keep = n < count
        turned_re = jnp.where(keep, real * cosine + imag * sine, 0.0)
        turned_im = jnp.where(keep, imag * cosine - real * sine, 0.0)
        return interleave(turned_re, turned_im).astype(jnp.bfloat16), interleave(-turned_im, turned_re).astype(jnp.bfloat16)

    def one_chunk(c, carry):
        first = one_slot(2 * c)
        second = one_slot(2 * c + 1)
        for ref, k in ((slots_re, 0), (slots_im, 1)):
            ref[c, :, :BR] = first[k]
            ref[c, :, BR:] = second[k]
        return carry

    lax.fori_loop(0, CHUNKS, one_chunk, 0)
    total[...] = jnp.zeros_like(total)

    def multiply(c, carry):
        matrix_copy(c).wait()
        total[...] += jnp.dot(slots_re[c], matrix_v[c, 0], preferred_element_type=jnp.float32) + jnp.dot(
            slots_im[c], matrix_v[c, 1], preferred_element_type=jnp.float32
        )
        return carry

    lax.fori_loop(0, CHUNKS, multiply, 0)
    for d in range(N_LINE):
        for depth in range(TZ):
            out_ref[d, depth] = total[16 * d : 16 * d + 16, TX * depth : TX * depth + TX].astype(jnp.bfloat16)


def partial_image(where, own, one, three, two, tables, beam_matrix):
    any_space = pl.BlockSpec(memory_space=pl.ANY)
    return pl.pallas_call(
        image_kernel,
        out_shape=jax.ShapeDtypeStruct((N_LINE, TZ, 16, TX), jnp.bfloat16),
        in_specs=[pl.BlockSpec(memory_space=pltpu.SMEM)]
        + [any_space] * 4
        + [pl.BlockSpec(memory_space=pltpu.VMEM), any_space],
        out_specs=pl.BlockSpec(memory_space=pltpu.VMEM),
        scratch_shapes=[
            pltpu.VMEM((N_TILE, ROWS, WIN), jnp.bfloat16),
            pltpu.VMEM((N_TILE, S, BR), jnp.float32),
            pltpu.VMEM((N_TILE, S, BR), jnp.float32),
            pltpu.VMEM((CHUNKS, 2 * S, CHUNK), jnp.bfloat16),
            pltpu.VMEM((CHUNKS, 2 * S, CHUNK), jnp.bfloat16),
            pltpu.VMEM((2 * S, TZ * TX), jnp.float32),
            pltpu.VMEM((MAXB + 8, WIN), jnp.int32),
            pltpu.SMEM((MAXB + 8, WIN), jnp.int32),
            pltpu.VMEM((CHUNKS, 2, CHUNK, TZ * TX), jnp.bfloat16),
            pltpu.SemaphoreType.DMA((4,)),
            pltpu.SemaphoreType.DMA((CHUNKS,)),
            pltpu.SemaphoreType.DMA,
        ],
        compiler_params=pltpu.CompilerParams(vmem_limit_bytes=40 * 2**20),
        name="partial_image",
    )(where, own, one, three, two, tables, beam_matrix)


def sum_kernel(parts_ref, out_ref, top_ref, bottom_ref):
    for depth in range(TZ):
        total = parts_ref[0, depth].astype(jnp.float32)
        for line in range(1, N_LINE):
            total = total + parts_ref[line, depth].astype(jnp.float32)
        out_ref[depth] = total
        if depth < 2:
            top_ref[depth] = total
        if depth >= TZ - 2:
            bottom_ref[depth - TZ + 2] = total


def summed_lines(parts):
    shapes = [jax.ShapeDtypeStruct((rows, 16, TX), jnp.float32) for rows in (TZ, 2, 2)]
    return pl.pallas_call(
        sum_kernel,
        out_shape=shapes,
        in_specs=[pl.BlockSpec(memory_space=pltpu.VMEM)],
        out_specs=[pl.BlockSpec(memory_space=pltpu.VMEM)] * 3,
        compiler_params=pltpu.CompilerParams(vmem_limit_bytes=8 * 2**20),
        name="summed_lines",
    )(parts)


def dip_kernel(filter_ref, above_ref, image_ref, below_ref, out_ref):
    rows = [above_ref[0], above_ref[1]] + [image_ref[d] for d in range(TZ)] + [below_ref[0], below_ref[1]]
    lane = lax.broadcasted_iota(jnp.int32, (16, TX), 1)
    results = [jnp.zeros((16, TX), jnp.float32) for _ in range(TZ)]
    for side in range(5):
        move = side - 2
        for source in range(TZ + 4):
            row = rows[source]
            if move:
                inside = (lane + move >= 0) & (lane + move < TX)
                row = jnp.where(inside, pltpu.roll(row, (-move) % TX, 1), 0.0)
            for depth in range(max(0, source - 4), min(TZ, source + 1)):
                results[depth] = results[depth] + filter_ref[source - depth, side] * row
    for depth in range(TZ):
        for part in range(2):
            out_ref[pl.ds(part * 64 + depth, 8, stride=TZ), :] = results[depth][8 * part : 8 * part + 8]


def dip_filtered(dip_filter, above, image, below):
    vmem = pl.BlockSpec(memory_space=pltpu.VMEM)
    return pl.pallas_call(
        dip_kernel,
        out_shape=jax.ShapeDtypeStruct((2 * 8 * TZ, TX), jnp.float32),
        in_specs=[pl.BlockSpec(memory_space=pltpu.SMEM), vmem, vmem, vmem],
        out_specs=vmem,
        compiler_params=pltpu.CompilerParams(vmem_limit_bytes=8 * 2**20),
        name="dip_filtered",
    )(dip_filter, above, image, below)


def per_device(traces, codes, routes, beam_matrix, dip_filter):
    line, tile = lax.axis_index("line"), lax.axis_index("tile")
    where = jnp.stack([tile, tile // SIDE, tile % SIDE, line % 2]).astype(jnp.int32)
    local = traces[0]
    rim = lax.ppermute(local[:HALF], "line", [(i + 1, i) for i in range(N_LINE - 1)])
    routes_row = jnp.pad(routes.astype(jnp.bfloat16), ((0, 0), (0, WIN - NB)))
    codes_row = jnp.pad(codes.astype(jnp.bfloat16), ((0, 0), (0, WIN - S)))
    aux = jnp.concatenate([routes_row, codes_row, jnp.zeros((14, WIN), jnp.bfloat16)], 0)
    tables = slant_tables()
    own = jnp.concatenate([local, rim, aux], 0)
    near = [own] + [lax.ppermute(own, BOTH, hops(o, False)) for o in RING[1:]]
    stack = jnp.stack(near)
    far = [lax.ppermute(stack, BOTH, hops(o, True)) for o in RING[1:]]
    partial = partial_image(where, stack, *far, tables, beam_matrix)
    parts = lax.all_to_all(partial, "line", 0, 0, tiled=True)
    image, top, bottom = summed_lines(parts)
    above = lax.ppermute(bottom, "tile", [(i, i + 1) for i in range(N_TILE - 1)])
    below = lax.ppermute(top, "tile", [(i + 1, i) for i in range(N_TILE - 1)])
    return dip_filtered(dip_filter, above, image, below).reshape(2, 8, TZ, TX)


def solution(mesh):
    in_specs = (
        P("tile", "line", None),
        P("tile", None),
        P("line", "tile"),
        P("line", "tile", None, None, None),
        P(),
    )
    out_specs = P(None, "line", "tile", None)
    return jax.shard_map(per_device, mesh=mesh, in_specs=in_specs, out_specs=out_specs, check_vma=False)
```

```python
import functools

import jax
import jax.numpy as jnp
from jax import lax
from jax.experimental import pallas as pl
from jax.experimental.pallas import tpu as pltpu
from jax.sharding import PartitionSpec as P


S = 64
P_SIZE = 256
WIN = 128
BR = 128
TZ = 8
TX = 128
MAXB = 32
NB = 16
HALF = WIN // 2
SIDE = 4
RING = (0, 1, 3, 2)
BOTH = ("line", "tile")
N_LINE = 8
N_TILE = 16
PAIR = 2 * BR
WIDE = TZ * TX
STREAMS = 16


def hops(offset, x_first):
    pairs = []
    for line in range(N_LINE):
        along_x = x_first == (line % 2 == 0)
        for x in range(SIDE):
            for z in range(SIDE):
                to_x, to_z = ((x + offset) % SIDE, z) if along_x else (x, (z + offset) % SIDE)
                pairs.append((line * N_TILE + x * SIDE + z, line * N_TILE + to_x * SIDE + to_z))
    return pairs


def prepare_kernel(matrix_ref, table_ref, held_ref, sems):
    copies = []
    for k in range(2):
        for part in range(STREAMS // 2):
            rows = pl.ds(part * (2 * MAXB * BR // STREAMS), 2 * MAXB * BR // STREAMS)
            copies.append(
                pltpu.make_async_copy(
                    matrix_ref.at[0, 0, k, rows, :], held_ref.at[k, rows, :], sems.at[len(copies)]
                )
            )
    for copy in copies:
        copy.start()
    rows = lax.broadcasted_iota(jnp.int32, (WIN, P_SIZE), 0)
    cols = lax.broadcasted_iota(jnp.int32, (WIN, P_SIZE), 1)
    turns = (cols - P_SIZE // 2) * (2 * rows - (WIN - 1))
    unit = 2.0 * jnp.pi / 8192.0
    step = (((turns + 4096) & 8191) - 4096).astype(jnp.float32) * unit
    base = (((32 * turns + 4096) & 8191) - 4096).astype(jnp.float32) * unit
    offsets = lax.broadcasted_iota(jnp.int32, (WIN, 1), 0).astype(jnp.float32) - (WIN - 1) / 2
    taper = jnp.exp(-0.5 * (offsets / (0.4 * WIN)) ** 2)
    taper = taper / jnp.sqrt(jnp.sum(taper * taper, axis=0, keepdims=True))
    step_c, step_s = jnp.cos(step), jnp.sin(step)
    now_c, now_s = taper * jnp.cos(base), -taper * jnp.sin(base)
    for f in range(N_TILE):
        for q in range(2):
            half = slice(q * BR, (q + 1) * BR)
            table_ref[2 * f + q, :, :BR] = now_c[:, half].astype(jnp.bfloat16)
            table_ref[2 * f + q, :, BR:] = now_s[:, half].astype(jnp.bfloat16)
        now_c, now_s = now_c * step_c + now_s * step_s, now_s * step_c - now_c * step_s
    for copy in copies:
        copy.wait()


def prepared(beam_matrix):
    return pl.pallas_call(
        prepare_kernel,
        out_shape=[
            pltpu.VMEM((2 * N_TILE, WIN, 2 * BR), jnp.bfloat16),
            pltpu.VMEM((2, MAXB * BR, WIDE), jnp.bfloat16),
        ],
        in_specs=[pl.BlockSpec(memory_space=pltpu.HBM)],
        out_specs=[pl.BlockSpec(memory_space=pltpu.VMEM)] * 2,
        scratch_shapes=[pltpu.SemaphoreType.DMA((STREAMS,))],
        compiler_params=pltpu.CompilerParams(vmem_limit_bytes=4 * 2**20),
        name="prepared",
    )(pltpu.with_memory_space_constraint(beam_matrix, pltpu.HBM))


def offset_of(place):
    return jnp.where(place == 3, 2, jnp.where(place == 2, 3, place))


def plan_kernel(own_ref, one_ref, three_ref, two_ref, plan_ref, cos_ref, sin_ref):
    tile = lax.axis_index("tile")
    x, z, parity = tile >> 2, tile & 3, lax.axis_index("line") & 1
    rows = [ref[i, :8, :].astype(jnp.float32) for ref in (own_ref, one_ref, three_ref, two_ref) for i in range(SIDE)]
    routes = jnp.concatenate([row[0:1] for row in rows], 0)
    codes = jnp.concatenate([row[1:2] for row in rows], 0)

    def sender(place):
        far, near = offset_of(place >> 2), offset_of(place & 3)
        dx, dz = jnp.where(parity == 0, far, near), jnp.where(parity == 0, near, far)
        return (((x - dx) & 3) << 2) + ((z - dz) & 3)

    wide = (N_TILE, WIN)
    place_r, lane = lax.broadcasted_iota(jnp.int32, wide, 0), lax.broadcasted_iota(jnp.int32, wide, 1)
    sender_r = sender(place_r)
    mine = jnp.where((lane < NB) & (routes == tile.astype(jnp.float32)), 1.0, 0.0)
    lane_r, lane_c = (lax.broadcasted_iota(jnp.int32, (WIN, WIN), axis) for axis in (0, 1))
    before_b = jnp.dot(mine, jnp.where(lane_r < lane_c, 1.0, 0.0), preferred_element_type=jnp.float32)
    counts = jnp.dot(mine, jnp.ones((WIN, WIN), jnp.float32), preferred_element_type=jnp.float32)
    place_a, place_b = (lax.broadcasted_iota(jnp.int32, (N_TILE, N_TILE), axis) for axis in (0, 1))
    earlier = jnp.where(sender(place_b) < sender(place_a), 1.0, 0.0)
    before_sender = jnp.dot(earlier, counts, preferred_element_type=jnp.float32)
    before_place = jnp.dot(jnp.where(place_b < place_a, 1.0, 0.0), counts, preferred_element_type=jnp.float32)
    slot = before_sender + before_b
    spot = jnp.where(mine > 0.0, before_place + before_b, -1.0)
    entry = slot * 1024.0 + ((place_r & 3) * 256 + sender_r * NB + lane).astype(jnp.float32)
    lane_f = lane.astype(jnp.float32)
    entries = jnp.zeros(wide, jnp.float32)
    for b in range(NB):
        entries = entries + jnp.where(spot[:, b : b + 1] == lane_f, entry[:, b : b + 1], 0.0)
    starts = jnp.where(place_r == 4 * lane, before_place, 0.0) + jnp.where(lane == SIDE, counts, 0.0)
    both = [jnp.sum(v, 0, keepdims=True) for v in (entries, starts)]
    plan_ref[...] = jnp.concatenate(both + [jnp.zeros((6, WIN), jnp.float32)], 0).astype(jnp.int32)

    code_cols = jnp.concatenate([codes, jnp.zeros((WIN - N_TILE, WIN), jnp.float32)], 0).T[:S]
    angles = code_cols * (2.0 * jnp.pi / 256.0)
    cosines, sines = jnp.cos(angles), jnp.sin(angles)
    for place in range(N_TILE):
        cos_ref[place] = jnp.broadcast_to(cosines[:, place : place + 1], (S, BR))
        sin_ref[place] = jnp.broadcast_to(sines[:, place : place + 1], (S, BR))


def planned(own, one, three, two):
    vmem = pl.BlockSpec(memory_space=pltpu.VMEM)
    turn = jax.ShapeDtypeStruct((N_TILE, S, BR), jnp.float32)
    return pl.pallas_call(
        plan_kernel,
        out_shape=[jax.ShapeDtypeStruct((8, WIN), jnp.int32), turn, turn],
        in_specs=[vmem] * 4,
        out_specs=[vmem] * 3,
        compiler_params=pltpu.CompilerParams(vmem_limit_bytes=8 * 2**20),
        name="planned",
    )(own, one, three, two)


def interleave(real, imag):
    pieces = []
    for d in range(N_LINE):
        pieces += [real[8 * d : 8 * d + 8], imag[8 * d : 8 * d + 8]]
    return jnp.concatenate(pieces, 0)


def image_kernel(phase, plan_ref, main_ref, cos_ref, sin_ref, table_ref, held_ref, *rest):
    first, last = phase == 0, phase == SIDE - 1
    if first:
        out_ref, slots = rest
    else:
        before_ref, out_ref, slots = rest
    start, end = plan_ref[1, phase], plan_ref[1, phase + 1]
    pairs = (end - start + 1) >> 1

    def one_slot(n):
        entry = plan_ref[0, jnp.minimum(n, MAXB - 1)]
        i, f, b = (entry >> 8) & 3, (entry >> 4) & 15, entry & 15
        window = main_ref[i, pl.ds(pl.multiple_of((b >> 1) * HALF, HALF), WIN), :]
        stacked = lax.dot_general(
            window, table_ref[2 * f + (b & 1)], (((0,), (0,)), ((), ())), preferred_element_type=jnp.float32
        )
        real = stacked[:S, :BR] - stacked[S:, BR:]
        imag = stacked[S:, :BR] + stacked[:S, BR:]
        cosine, sine = cos_ref[SIDE * phase + i], sin_ref[SIDE * phase + i]
        keep = n < end
        turned_re = jnp.where(keep, real * cosine + imag * sine, 0.0)
        turned_im = jnp.where(keep, imag * cosine - real * sine, 0.0)
        return interleave(turned_re, turned_im).astype(jnp.bfloat16), interleave(-turned_im, turned_re).astype(jnp.bfloat16)

    def make_pair(c, carry):
        for k in range(2):
            plain, crossed = one_slot(start + 2 * c + k)
            slots[c, :, k * BR : (k + 1) * BR] = plain
            slots[c, :, PAIR + k * BR : PAIR + (k + 1) * BR] = crossed
        return carry

    lax.fori_loop(0, pairs, make_pair, 0)
    total = out_ref if not last else before_ref
    if first:
        out_ref[...] = jnp.zeros_like(out_ref)
    elif not last:
        out_ref[...] = before_ref[...]

    def multiply(c, carry):
        at = []
        for k in range(2):
            slot = plan_ref[0, jnp.minimum(start + 2 * c + k, MAXB - 1)] >> 10
            at.append(pl.ds(pl.multiple_of(slot * BR, BR), BR))
        matrix = jnp.concatenate([held_ref[k, rows, :] for k in range(2) for rows in at], 0)
        total[...] += jnp.dot(slots[c], matrix, preferred_element_type=jnp.float32)
        return carry

    lax.fori_loop(0, pairs, multiply, 0)
    if last:
        for d in range(N_LINE):
            for depth in range(TZ):
                out_ref[d, depth] = total[16 * d : 16 * d + 16, TX * depth : TX * depth + TX].astype(jnp.bfloat16)


def image_part(phase, plan, main, turns, tables, held, before):
    smem, vmem = pl.BlockSpec(memory_space=pltpu.SMEM), pl.BlockSpec(memory_space=pltpu.VMEM)
    last = phase == SIDE - 1
    fixed = [pltpu.with_memory_space_constraint(v, pltpu.VMEM) for v in (main, *turns, tables, held)]
    earlier = () if before is None else (pltpu.with_memory_space_constraint(before, pltpu.VMEM),)
    shape = (N_LINE, TZ, 16, TX) if last else (2 * S, WIDE)
    return pl.pallas_call(
        functools.partial(image_kernel, phase),
        out_shape=pltpu.VMEM(shape, jnp.bfloat16 if last else jnp.float32),
        in_specs=[smem] + [vmem] * (5 + len(earlier)),
        out_specs=vmem,
        scratch_shapes=[pltpu.VMEM((MAXB // 4, 2 * S, 2 * PAIR), jnp.bfloat16)],
        input_output_aliases={} if last or before is None else {6: 0},
        compiler_params=pltpu.CompilerParams(vmem_limit_bytes=6 * 2**20),
        cost_estimate=pl.CostEstimate(flops=2 * 8 * 2 * S * 2 * BR * WIDE, bytes_accessed=2**20, transcendentals=0),
    )(plan, *fixed, *earlier)


def sum_kernel(parts_ref, out_ref, top_ref, bottom_ref):
    for depth in range(TZ):
        total = parts_ref[0, depth].astype(jnp.float32)
        for line in range(1, N_LINE):
            total = total + parts_ref[line, depth].astype(jnp.float32)
        out_ref[depth] = total
        if depth < 2:
            top_ref[depth] = total
        if depth >= TZ - 2:
            bottom_ref[depth - TZ + 2] = total


def summed_lines(parts):
    shapes = [jax.ShapeDtypeStruct((rows, 16, TX), jnp.float32) for rows in (TZ, 2, 2)]
    return pl.pallas_call(
        sum_kernel,
        out_shape=shapes,
        in_specs=[pl.BlockSpec(memory_space=pltpu.VMEM)],
        out_specs=[pl.BlockSpec(memory_space=pltpu.VMEM)] * 3,
        compiler_params=pltpu.CompilerParams(vmem_limit_bytes=8 * 2**20),
        name="summed_lines",
    )(parts)


def dip_kernel(filter_ref, above_ref, image_ref, below_ref, out_ref):
    rows = [above_ref[0], above_ref[1]] + [image_ref[d] for d in range(TZ)] + [below_ref[0], below_ref[1]]
    lane = lax.broadcasted_iota(jnp.int32, (16, TX), 1)
    results = [jnp.zeros((16, TX), jnp.float32) for _ in range(TZ)]
    for side in range(5):
        move = side - 2
        for source in range(TZ + 4):
            row = rows[source]
            if move:
                inside = (lane + move >= 0) & (lane + move < TX)
                row = jnp.where(inside, pltpu.roll(row, (-move) % TX, 1), 0.0)
            for depth in range(max(0, source - 4), min(TZ, source + 1)):
                results[depth] = results[depth] + filter_ref[source - depth, side] * row
    for depth in range(TZ):
        for part in range(2):
            out_ref[pl.ds(part * 64 + depth, 8, stride=TZ), :] = results[depth][8 * part : 8 * part + 8]


def dip_filtered(dip_filter, above, image, below):
    vmem = pl.BlockSpec(memory_space=pltpu.VMEM)
    return pl.pallas_call(
        dip_kernel,
        out_shape=jax.ShapeDtypeStruct((2 * 8 * TZ, TX), jnp.float32),
        in_specs=[pl.BlockSpec(memory_space=pltpu.SMEM), vmem, vmem, vmem],
        out_specs=vmem,
        compiler_params=pltpu.CompilerParams(vmem_limit_bytes=8 * 2**20),
        name="dip_filtered",
    )(dip_filter, above, image, below)


def spread(value, x_first):
    return [lax.ppermute(value, BOTH, hops(offset, x_first)) for offset in RING[1:]]


def per_device(traces, codes, routes, beam_matrix, dip_filter):
    local = traces[0]
    rim = lax.ppermute(local[:HALF], "line", [(i + 1, i) for i in range(N_LINE - 1)])
    routes_row = jnp.pad(routes.astype(jnp.bfloat16), ((0, 0), (0, WIN - NB)))
    codes_row = jnp.pad(codes.astype(jnp.bfloat16), ((0, 0), (0, WIN - S)))
    aux = jnp.concatenate([routes_row, codes_row, jnp.zeros((14, WIN), jnp.bfloat16)], 0)
    near_aux = jnp.stack([aux] + spread(aux, False))
    main = jnp.concatenate([local, rim], 0)
    near_main = jnp.stack([main] + spread(main, False))
    all_aux = [near_aux] + spread(near_aux, True)
    mains = [near_main] + spread(near_main, True)
    tables, held = prepared(beam_matrix)
    plan, *turns = planned(*all_aux)
    image = None
    for phase in range(SIDE):
        image = image_part(phase, plan, mains[phase], turns, tables, held, image)
    parts = lax.all_to_all(image, "line", 0, 0, tiled=True)
    image, top, bottom = summed_lines(parts)
    above = lax.ppermute(bottom, "tile", [(i, i + 1) for i in range(N_TILE - 1)])
    below = lax.ppermute(top, "tile", [(i + 1, i) for i in range(N_TILE - 1)])
    return dip_filtered(dip_filter, above, image, below).reshape(2, 8, TZ, TX)


def solution(mesh):
    in_specs = (
        P("tile", "line", None),
        P("tile", None),
        P("line", "tile"),
        P("line", "tile", None, None, None),
        P(),
    )
    out_specs = P(None, "line", "tile", None)

    return jax.shard_map(per_device, mesh=mesh, in_specs=in_specs, out_specs=out_specs, check_vma=False)
```

```python
import jax
import jax.numpy as jnp
from jax import lax
from jax.experimental import pallas as pl
from jax.experimental.pallas import tpu as pltpu
from jax.sharding import PartitionSpec as P


S = 64
P_SIZE = 256
WIN = 128
BR = 128
TZ = 8
TX = 128
MAXB = 32
NB = 16
HALF = WIN // 2
LOCAL = 512
ROWS = LOCAL + 16
SIDE = 4
RING = (0, 1, 3, 2)
BOTH = ("line", "tile")
N_LINE = 8
N_TILE = 16
QUAD = 4
STREAMS = 16
WIDE = TZ * TX


def hops(offset, x_first):
    pairs = []
    for line in range(N_LINE):
        along_x = x_first == (line % 2 == 0)
        for x in range(SIDE):
            for z in range(SIDE):
                to_x, to_z = ((x + offset) % SIDE, z) if along_x else (x, (z + offset) % SIDE)
                pairs.append((line * N_TILE + x * SIDE + z, line * N_TILE + to_x * SIDE + to_z))
    return pairs


def first_kernel(traces_ref, routes_ref, codes_ref, main_ref, rows, routes_v, codes_v, sems):
    copies = (
        pltpu.make_async_copy(traces_ref.at[0], main_ref.at[pl.ds(0, LOCAL)], sems.at[0]),
        pltpu.make_async_copy(routes_ref, routes_v, sems.at[1]),
        pltpu.make_async_copy(codes_ref, codes_v, sems.at[2]),
    )
    for copy in copies:
        copy.start()
    rows[...] = jnp.zeros_like(rows)
    for copy in copies:
        copy.wait()
    rows[0:1, :NB] = routes_v[...].astype(jnp.float32)
    rows[1:2, :S] = codes_v[...].astype(jnp.float32)
    main_ref[LOCAL:] = rows[...].astype(jnp.bfloat16)


def first_rows(traces, routes, codes):
    return pl.pallas_call(
        first_kernel,
        out_shape=pltpu.VMEM((ROWS, WIN), jnp.bfloat16),
        in_specs=[pl.BlockSpec(memory_space=pltpu.HBM)] * 3,
        out_specs=pl.BlockSpec(memory_space=pltpu.VMEM),
        scratch_shapes=[
            pltpu.VMEM((16, WIN), jnp.float32),
            pltpu.VMEM((1, NB), jnp.int32),
            pltpu.VMEM((1, S), jnp.int32),
            pltpu.SemaphoreType.DMA((3,)),
        ],
        compiler_params=pltpu.CompilerParams(vmem_limit_bytes=2 * 2**20),
        name="first_rows",
    )(*(pltpu.with_memory_space_constraint(v, pltpu.HBM) for v in (traces, routes, codes)))


def table_kernel(table_ref):
    rows = lax.broadcasted_iota(jnp.int32, (WIN, P_SIZE), 0)
    cols = lax.broadcasted_iota(jnp.int32, (WIN, P_SIZE), 1)
    turns = (cols - P_SIZE // 2) * (2 * rows - (WIN - 1))
    unit = 2.0 * jnp.pi / 8192.0
    step = (((turns + 4096) & 8191) - 4096).astype(jnp.float32) * unit
    base = (((32 * turns + 4096) & 8191) - 4096).astype(jnp.float32) * unit
    offsets = lax.broadcasted_iota(jnp.int32, (WIN, 1), 0).astype(jnp.float32) - (WIN - 1) / 2
    taper = jnp.exp(-0.5 * (offsets / (0.4 * WIN)) ** 2)
    taper = taper / jnp.sqrt(jnp.sum(taper * taper, axis=0, keepdims=True))
    step_c, step_s = jnp.cos(step), jnp.sin(step)
    now_c, now_s = taper * jnp.cos(base), -taper * jnp.sin(base)
    for f in range(N_TILE):
        for q in range(2):
            half = slice(q * BR, (q + 1) * BR)
            table_ref[2 * f + q, :, :BR] = now_c[:, half].astype(jnp.bfloat16)
            table_ref[2 * f + q, :, BR:] = now_s[:, half].astype(jnp.bfloat16)
        now_c, now_s = now_c * step_c + now_s * step_s, now_s * step_c - now_c * step_s


def slant_tables():
    return pl.pallas_call(
        table_kernel,
        out_shape=pltpu.VMEM((2 * N_TILE, WIN, 2 * BR), jnp.bfloat16),
        out_specs=pl.BlockSpec(memory_space=pltpu.VMEM),
        compiler_params=pltpu.CompilerParams(vmem_limit_bytes=4 * 2**20),
        name="slant_tables",
    )()


def hold_kernel(matrix_ref, held_ref, sems):
    copies = []
    for part in range(2):
        for piece in range(STREAMS // 2):
            rows = pl.ds(piece * (2 * MAXB * BR // STREAMS), 2 * MAXB * BR // STREAMS)
            source, target = matrix_ref.at[0, 0, part, rows, :], held_ref.at[part, rows, :]
            copies.append(pltpu.make_async_copy(source, target, sems.at[len(copies)]))
    for copy in copies:
        copy.start()
    for copy in copies:
        copy.wait()


def held_matrices(beam_matrix):
    return pl.pallas_call(
        hold_kernel,
        out_shape=pltpu.VMEM((2, MAXB * BR, WIDE), jnp.bfloat16),
        in_specs=[pl.BlockSpec(memory_space=pltpu.HBM)],
        out_specs=pl.BlockSpec(memory_space=pltpu.VMEM),
        scratch_shapes=[pltpu.SemaphoreType.DMA((STREAMS,))],
        compiler_params=pltpu.CompilerParams(vmem_limit_bytes=2 * 2**20),
        name="held_matrices",
    )(pltpu.with_memory_space_constraint(beam_matrix, pltpu.HBM))


def offset_of(place):
    return jnp.where(place == 3, 2, jnp.where(place == 2, 3, place))


def plan_kernel(own_ref, one_ref, three_ref, two_ref, plan_ref, cos_ref, sin_ref):
    tile = lax.axis_index("tile")
    x, z, parity = tile >> 2, tile & 3, lax.axis_index("line") & 1
    rows = [ref[i, LOCAL : LOCAL + 8, :].astype(jnp.float32) for ref in (own_ref, one_ref, three_ref, two_ref) for i in range(SIDE)]
    routes, codes = (jnp.concatenate([row[k : k + 1] for row in rows], 0) for k in range(2))

    def sender(place):
        far, near = offset_of(place >> 2), offset_of(place & 3)
        dx, dz = jnp.where(parity == 0, far, near), jnp.where(parity == 0, near, far)
        return (((x - dx) & 3) << 2) + ((z - dz) & 3)

    wide = (N_TILE, WIN)
    place_r, lane = lax.broadcasted_iota(jnp.int32, wide, 0), lax.broadcasted_iota(jnp.int32, wide, 1)
    sender_r = sender(place_r)
    mine = jnp.where((lane < NB) & (routes == tile.astype(jnp.float32)), 1.0, 0.0)
    lane_r, lane_c = (lax.broadcasted_iota(jnp.int32, (WIN, WIN), axis) for axis in (0, 1))
    before_b = jnp.dot(mine, jnp.where(lane_r < lane_c, 1.0, 0.0), preferred_element_type=jnp.float32)
    counts = jnp.dot(mine, jnp.ones((WIN, WIN), jnp.float32), preferred_element_type=jnp.float32)
    place_a, place_b = (lax.broadcasted_iota(jnp.int32, (N_TILE, N_TILE), axis) for axis in (0, 1))
    earlier = jnp.where(sender(place_b) < sender(place_a), 1.0, 0.0)
    before_sender = jnp.dot(earlier, counts, preferred_element_type=jnp.float32)
    before_place = jnp.dot(jnp.where(place_b < place_a, 1.0, 0.0), counts, preferred_element_type=jnp.float32)
    slot, spot = before_sender + before_b, before_place + before_b
    spot = jnp.where(mine > 0.0, spot, -1.0)
    entry = slot * 4096.0 + (place_r * 256 + sender_r * NB + lane).astype(jnp.float32)
    lane_f = lane.astype(jnp.float32)
    entries = jnp.zeros(wide, jnp.float32)
    for b in range(NB):
        entries = entries + jnp.where(spot[:, b : b + 1] == lane_f, entry[:, b : b + 1], 0.0)
    starts = jnp.where(place_r == SIDE * lane, before_place, 0.0) + jnp.where(lane == SIDE, counts, 0.0)
    starts = jnp.sum(starts, 0, keepdims=True)
    entries = jnp.sum(entries, 0, keepdims=True)
    plan_ref[...] = jnp.concatenate([entries, starts, jnp.zeros((6, WIN), jnp.float32)], 0).astype(jnp.int32)

    code_cols = jnp.concatenate([codes, jnp.zeros((WIN - N_TILE, WIN), jnp.float32)], 0).T[:S]
    angles = code_cols * (2.0 * jnp.pi / 256.0)
    cosines, sines = jnp.cos(angles), jnp.sin(angles)
    for place in range(N_TILE):
        cos_ref[place] = jnp.broadcast_to(cosines[:, place : place + 1], (S, BR))
        sin_ref[place] = jnp.broadcast_to(sines[:, place : place + 1], (S, BR))


def planned(*mains):
    vmem = pl.BlockSpec(memory_space=pltpu.VMEM)
    turn = jax.ShapeDtypeStruct((N_TILE, S, BR), jnp.float32)
    return pl.pallas_call(
        plan_kernel,
        out_shape=[jax.ShapeDtypeStruct((8, WIN), jnp.int32), turn, turn],
        in_specs=[vmem] * SIDE,
        out_specs=[vmem] * 3,
        compiler_params=pltpu.CompilerParams(vmem_limit_bytes=8 * 2**20),
        name="planned",
    )(*(pltpu.with_memory_space_constraint(v, pltpu.VMEM) for v in mains))


def interleave(real, imag):
    pieces = []
    for d in range(N_LINE):
        pieces += [real[8 * d : 8 * d + 8], imag[8 * d : 8 * d + 8]]
    return jnp.concatenate(pieces, 0)


def image_kernel(plan_ref, *refs):
    main_refs = refs[:SIDE]
    rim_ref, cos_ref, sin_ref, table_ref, held_ref, out_ref, slots_re, slots_im, total = refs[SIDE:]
    count = plan_ref[1, SIDE]

    def make_slot(group, n):
        entry = plan_ref[0, jnp.minimum(n, MAXB - 1)]
        place, f, b = (entry >> 8) & 15, (entry >> 4) & 15, entry & 15
        w, i, main_ref = b >> 1, place & 3, main_refs[group]
        head = main_ref[i, pl.ds(pl.multiple_of(w * HALF, HALF), HALF), :]
        tail = main_ref[i, pl.ds(pl.multiple_of(jnp.minimum(w + 1, 7) * HALF, HALF), HALF), :]
        window = jnp.concatenate([head, jnp.where(w == 7, rim_ref[i, group], tail)], 0)
        stacked = lax.dot_general(
            window, table_ref[2 * f + (b & 1)], (((0,), (0,)), ((), ())), preferred_element_type=jnp.float32
        )
        real = stacked[:S, :BR] - stacked[S:, BR:]
        imag = stacked[S:, :BR] + stacked[:S, BR:]
        cosine, sine = cos_ref[SIDE * group + i], sin_ref[SIDE * group + i]
        turned_re = real * cosine + imag * sine
        turned_im = imag * cosine - real * sine
        return interleave(turned_re, turned_im).astype(jnp.bfloat16), interleave(-turned_im, turned_re).astype(jnp.bfloat16)

    for group in range(SIDE):
        start, end = plan_ref[1, group], plan_ref[1, group + 1]

        def make_quad(c, carry, group=group, start=start):
            made = [make_slot(group, start + QUAD * c + k) for k in range(QUAD)]
            for k in range(QUAD):
                slots_re[start + QUAD * c + k], slots_im[start + QUAD * c + k] = made[k]
            return carry

        lax.fori_loop(0, (end - start + QUAD - 1) >> 2, make_quad, 0)
    for k in range(QUAD):
        slots_re[count + k] = jnp.zeros((2 * S, BR), jnp.bfloat16)
        slots_im[count + k] = jnp.zeros((2 * S, BR), jnp.bfloat16)
    total[...] = jnp.zeros_like(total)

    def multiply(c, carry):
        at = []
        for k in range(QUAD):
            slot = plan_ref[0, jnp.minimum(QUAD * c + k, count - 1)] >> 12
            at.append(pl.ds(pl.multiple_of(slot * BR, BR), BR))
        matrix = jnp.concatenate([held_ref[part, rows, :] for part in range(2) for rows in at], 0)
        beams = [ref[QUAD * c + k] for ref in (slots_re, slots_im) for k in range(QUAD)]
        total[...] += jnp.dot(jnp.concatenate(beams, 1), matrix, preferred_element_type=jnp.float32)
        return carry

    lax.fori_loop(0, (count + QUAD - 1) >> 2, multiply, 0)
    for d in range(N_LINE):
        for depth in range(TZ):
            out_ref[d, depth] = total[16 * d : 16 * d + 16, TX * depth : TX * depth + TX].astype(jnp.bfloat16)


def partial_image(plan, mains, rims, turns, tables, held):
    smem, vmem = pl.BlockSpec(memory_space=pltpu.SMEM), pl.BlockSpec(memory_space=pltpu.VMEM)
    fixed = [pltpu.with_memory_space_constraint(v, pltpu.VMEM) for v in (*mains, rims, *turns, tables, held)]
    room = MAXB + QUAD * 2
    return pl.pallas_call(
        image_kernel,
        out_shape=pltpu.VMEM((N_LINE, TZ, 16, TX), jnp.bfloat16),
        in_specs=[smem] + [vmem] * len(fixed),
        out_specs=vmem,
        scratch_shapes=[
            pltpu.VMEM((room, 2 * S, BR), jnp.bfloat16),
            pltpu.VMEM((room, 2 * S, BR), jnp.bfloat16),
            pltpu.VMEM((2 * S, WIDE), jnp.float32),
        ],
        compiler_params=pltpu.CompilerParams(vmem_limit_bytes=6 * 2**20),
        name="partial_image",
    )(plan, *fixed)


def sum_kernel(parts_ref, out_ref, top_ref, bottom_ref):
    for depth in range(TZ):
        total = parts_ref[0, depth].astype(jnp.float32)
        for line in range(1, N_LINE):
            total = total + parts_ref[line, depth].astype(jnp.float32)
        out_ref[depth] = total
        if depth < 2:
            top_ref[depth] = total
        if depth >= TZ - 2:
            bottom_ref[depth - TZ + 2] = total


def summed_lines(parts):
    shapes = [jax.ShapeDtypeStruct((rows, 16, TX), jnp.float32) for rows in (TZ, 2, 2)]
    return pl.pallas_call(
        sum_kernel,
        out_shape=shapes,
        in_specs=[pl.BlockSpec(memory_space=pltpu.VMEM)],
        out_specs=[pl.BlockSpec(memory_space=pltpu.VMEM)] * 3,
        compiler_params=pltpu.CompilerParams(vmem_limit_bytes=8 * 2**20),
        name="summed_lines",
    )(parts)


def add_filtered(filter_ref, results, sources):
    lane = lax.broadcasted_iota(jnp.int32, (16, TX), 1)
    for side in range(5):
        move = side - 2
        inside = (lane + move >= 0) & (lane + move < TX)
        for source, row in sources:
            if move:
                row = jnp.where(inside, pltpu.roll(row, (-move) % TX, 1), 0.0)
            for depth in range(max(0, source - 4), min(TZ, source + 1)):
                results[depth] = results[depth] + filter_ref[source - depth, side] * row
    return results


def inner_kernel(filter_ref, image_ref, out_ref):
    results = [jnp.zeros((16, TX), jnp.float32) for _ in range(TZ)]
    results = add_filtered(filter_ref, results, [(depth + 2, image_ref[depth]) for depth in range(TZ)])
    for depth in range(TZ):
        out_ref[depth] = results[depth]


def outer_kernel(filter_ref, above_ref, inner_ref, below_ref, out_ref):
    sources = [(0, above_ref[0]), (1, above_ref[1]), (TZ + 2, below_ref[0]), (TZ + 3, below_ref[1])]
    results = add_filtered(filter_ref, [inner_ref[depth] for depth in range(TZ)], sources)
    for depth in range(TZ):
        for part in range(2):
            out_ref[pl.ds(part * 64 + depth, 8, stride=TZ), :] = results[depth][8 * part : 8 * part + 8]


def dip_call(kernel, shape, dip_filter, *arrays):
    vmem = pl.BlockSpec(memory_space=pltpu.VMEM)
    return pl.pallas_call(
        kernel,
        out_shape=jax.ShapeDtypeStruct(shape, jnp.float32),
        in_specs=[pl.BlockSpec(memory_space=pltpu.SMEM)] + [vmem] * len(arrays),
        out_specs=vmem,
        compiler_params=pltpu.CompilerParams(vmem_limit_bytes=2 * 2**20),
    )(dip_filter, *arrays)


def spread(value, x_first, offsets=RING[1:]):
    received = []
    for offset in offsets:
        received.append(lax.ppermute(value, BOTH, hops(offset, x_first)))
    return received


def per_device(traces, codes, routes, beam_matrix, dip_filter):
    main = first_rows(traces, routes, codes)
    near = jnp.stack([main] + spread(main, False))
    mains = [near] + spread(near, True)
    plan, *turns = planned(*mains)
    tables = slant_tables()
    rim = lax.ppermute(near[:, :HALF], "line", [(i + 1, i) for i in range(N_LINE - 1)])
    rims = jnp.stack([rim] + spread(rim, False))
    held = held_matrices(beam_matrix)
    image = partial_image(plan, mains, rims, turns, tables, held)
    parts = lax.all_to_all(image, "line", 0, 0, tiled=True)
    image, top, bottom = summed_lines(parts)
    inner = dip_call(inner_kernel, (TZ, 16, TX), dip_filter, image)
    above = lax.ppermute(bottom, "tile", [(i, i + 1) for i in range(N_TILE - 1)])
    below = lax.ppermute(top, "tile", [(i + 1, i) for i in range(N_TILE - 1)])
    return dip_call(outer_kernel, (2 * 8 * TZ, TX), dip_filter, above, inner, below).reshape(2, 8, TZ, TX)


def solution(mesh):
    in_specs = (
        P("tile", "line", None),
        P("tile", None),
        P("line", "tile"),
        P("line", "tile", None, None, None),
        P(),
    )
    out_specs = P(None, "line", "tile", None)

    return jax.shard_map(per_device, mesh=mesh, in_specs=in_specs, out_specs=out_specs, check_vma=False)
```

```python
import jax
import jax.numpy as jnp
from jax import lax
from jax.experimental import pallas as pl
from jax.experimental.pallas import tpu as pltpu
from jax.sharding import PartitionSpec as P


S = 64
P_SIZE = 256
WIN = 128
BR = 128
TZ = 8
TX = 128
MAXB = 32
NB = 16
HALF = WIN // 2
LOCAL = 512
ROWS = LOCAL + 16
SIDE = 4
RING = (0, 1, 3, 2)
BOTH = ("line", "tile")
N_LINE = 8
N_TILE = 16
QUAD = 4
PIECES = (0, 1792, 2816, MAXB * BR)
STREAMS = 4
WIDE = TZ * TX


def hops(offset, x_first):
    pairs = []
    for line in range(N_LINE):
        along_x = x_first == (line % 2 == 0)
        for x in range(SIDE):
            for z in range(SIDE):
                to_x, to_z = ((x + offset) % SIDE, z) if along_x else (x, (z + offset) % SIDE)
                pairs.append((line * N_TILE + x * SIDE + z, line * N_TILE + to_x * SIDE + to_z))
    return pairs


def first_kernel(traces_ref, routes_ref, codes_ref, main_ref, rows, routes_v, codes_v, sems):
    copies = (
        pltpu.make_async_copy(traces_ref.at[0], main_ref.at[pl.ds(0, LOCAL)], sems.at[0]),
        pltpu.make_async_copy(routes_ref, routes_v, sems.at[1]),
        pltpu.make_async_copy(codes_ref, codes_v, sems.at[2]),
    )
    for copy in copies:
        copy.start()
    rows[...] = jnp.zeros_like(rows)
    for copy in copies:
        copy.wait()
    rows[0:1, :NB] = routes_v[...].astype(jnp.float32)
    rows[1:2, :S] = codes_v[...].astype(jnp.float32)
    main_ref[LOCAL:] = rows[...].astype(jnp.bfloat16)


def first_rows(traces, routes, codes):
    return pl.pallas_call(
        first_kernel,
        out_shape=pltpu.VMEM((ROWS, WIN), jnp.bfloat16),
        in_specs=[pl.BlockSpec(memory_space=pltpu.HBM)] * 3,
        out_specs=pl.BlockSpec(memory_space=pltpu.VMEM),
        scratch_shapes=[
            pltpu.VMEM((16, WIN), jnp.float32),
            pltpu.VMEM((1, NB), jnp.int32),
            pltpu.VMEM((1, S), jnp.int32),
            pltpu.SemaphoreType.DMA((3,)),
        ],
        compiler_params=pltpu.CompilerParams(vmem_limit_bytes=2 * 2**20),
        name="first_rows",
    )(*(pltpu.with_memory_space_constraint(v, pltpu.HBM) for v in (traces, routes, codes)))


def table_kernel(matrix_ref, table_ref, held_ref, sems):
    copies = piece_copies(0, matrix_ref, held_ref, sems)
    for copy in copies:
        copy.start()
    rows = lax.broadcasted_iota(jnp.int32, (WIN, P_SIZE), 0)
    cols = lax.broadcasted_iota(jnp.int32, (WIN, P_SIZE), 1)
    turns = (cols - P_SIZE // 2) * (2 * rows - (WIN - 1))
    unit = 2.0 * jnp.pi / 8192.0
    step = (((turns + 4096) & 8191) - 4096).astype(jnp.float32) * unit
    base = (((32 * turns + 4096) & 8191) - 4096).astype(jnp.float32) * unit
    offsets = lax.broadcasted_iota(jnp.int32, (WIN, 1), 0).astype(jnp.float32) - (WIN - 1) / 2
    taper = jnp.exp(-0.5 * (offsets / (0.4 * WIN)) ** 2)
    taper = taper / jnp.sqrt(jnp.sum(taper * taper, axis=0, keepdims=True))
    step_c, step_s = jnp.cos(step), jnp.sin(step)
    now_c, now_s = taper * jnp.cos(base), -taper * jnp.sin(base)
    for f in range(N_TILE):
        for q in range(2):
            half = slice(q * BR, (q + 1) * BR)
            table_ref[2 * f + q, :, :BR] = now_c[:, half].astype(jnp.bfloat16)
            table_ref[2 * f + q, :, BR:] = now_s[:, half].astype(jnp.bfloat16)
        now_c, now_s = now_c * step_c + now_s * step_s, now_s * step_c - now_c * step_s
    for copy in copies:
        copy.wait()


def slant_tables(beam_matrix):
    vmem = pl.BlockSpec(memory_space=pltpu.VMEM)
    return pl.pallas_call(
        table_kernel,
        out_shape=[
            pltpu.VMEM((2 * N_TILE, WIN, 2 * BR), jnp.bfloat16),
            pltpu.VMEM((2, MAXB * BR, WIDE), jnp.bfloat16),
        ],
        in_specs=[pl.BlockSpec(memory_space=pltpu.HBM)],
        out_specs=[vmem] * 2,
        scratch_shapes=[pltpu.SemaphoreType.DMA((2 * STREAMS,))],
        compiler_params=pltpu.CompilerParams(vmem_limit_bytes=4 * 2**20),
        name="slant_tables",
    )(pltpu.with_memory_space_constraint(beam_matrix, pltpu.HBM))


def piece_copies(piece, matrix_ref, held_ref, sems):
    copies = []
    first, rows = PIECES[piece], (PIECES[piece + 1] - PIECES[piece]) // STREAMS
    for part in range(2):
        for k in range(STREAMS):
            at = pl.ds(first + k * rows, rows)
            source, target = matrix_ref.at[0, 0, part, at, :], held_ref.at[part, at, :]
            copies.append(pltpu.make_async_copy(source, target, sems.at[len(copies)]))
    return copies


def hold_kernel(matrix_ref, before_ref, held_ref, sems):
    copies = piece_copies(1, matrix_ref, held_ref, sems)
    for copy in copies:
        copy.start()
    for copy in copies:
        copy.wait()


def held_more(beam_matrix, held):
    hbm, vmem = pl.BlockSpec(memory_space=pltpu.HBM), pl.BlockSpec(memory_space=pltpu.VMEM)
    return pl.pallas_call(
        hold_kernel,
        out_shape=pltpu.VMEM((2, MAXB * BR, WIDE), jnp.bfloat16),
        in_specs=[hbm, vmem],
        out_specs=vmem,
        scratch_shapes=[pltpu.SemaphoreType.DMA((2 * STREAMS,))],
        input_output_aliases={1: 0},
        compiler_params=pltpu.CompilerParams(vmem_limit_bytes=2 * 2**20),
        name="held_more",
    )(pltpu.with_memory_space_constraint(beam_matrix, pltpu.HBM), pltpu.with_memory_space_constraint(held, pltpu.VMEM))


def offset_of(place):
    return jnp.where(place == 3, 2, jnp.where(place == 2, 3, place))


def plan_kernel(own_ref, one_ref, three_ref, two_ref, plan_ref, cos_ref, sin_ref):
    tile = lax.axis_index("tile")
    x, z, parity = tile >> 2, tile & 3, lax.axis_index("line") & 1
    rows = [ref[i, LOCAL : LOCAL + 8, :].astype(jnp.float32) for ref in (own_ref, one_ref, three_ref, two_ref) for i in range(SIDE)]
    routes, codes = (jnp.concatenate([row[k : k + 1] for row in rows], 0) for k in range(2))

    def sender(place):
        far, near = offset_of(place >> 2), offset_of(place & 3)
        dx, dz = jnp.where(parity == 0, far, near), jnp.where(parity == 0, near, far)
        return (((x - dx) & 3) << 2) + ((z - dz) & 3)

    wide = (N_TILE, WIN)
    place_r, lane = lax.broadcasted_iota(jnp.int32, wide, 0), lax.broadcasted_iota(jnp.int32, wide, 1)
    sender_r = sender(place_r)
    mine = jnp.where((lane < NB) & (routes == tile.astype(jnp.float32)), 1.0, 0.0)
    lane_r, lane_c = (lax.broadcasted_iota(jnp.int32, (WIN, WIN), axis) for axis in (0, 1))
    before_b = jnp.dot(mine, jnp.where(lane_r < lane_c, 1.0, 0.0), preferred_element_type=jnp.float32)
    counts = jnp.dot(mine, jnp.ones((WIN, WIN), jnp.float32), preferred_element_type=jnp.float32)
    place_a, place_b = (lax.broadcasted_iota(jnp.int32, (N_TILE, N_TILE), axis) for axis in (0, 1))
    earlier = jnp.where(sender(place_b) < sender(place_a), 1.0, 0.0)
    before_sender = jnp.dot(earlier, counts, preferred_element_type=jnp.float32)
    before_place = jnp.dot(jnp.where(place_b < place_a, 1.0, 0.0), counts, preferred_element_type=jnp.float32)
    slot, spot = before_sender + before_b, before_place + before_b
    spot = jnp.where(mine > 0.0, spot, -1.0)
    entry = slot * 4096.0 + (place_r * 256 + sender_r * NB + lane).astype(jnp.float32)
    lane_f = lane.astype(jnp.float32)
    entries = jnp.zeros(wide, jnp.float32)
    for b in range(NB):
        entries = entries + jnp.where(spot[:, b : b + 1] == lane_f, entry[:, b : b + 1], 0.0)
    starts = jnp.where(place_r == SIDE * lane, before_place, 0.0) + jnp.where(lane == SIDE, counts, 0.0)
    starts = jnp.sum(starts, 0, keepdims=True)
    entries = jnp.sum(entries, 0, keepdims=True)
    plan_ref[...] = jnp.concatenate([entries, starts, jnp.zeros((6, WIN), jnp.float32)], 0).astype(jnp.int32)

    code_cols = jnp.concatenate([codes, jnp.zeros((WIN - N_TILE, WIN), jnp.float32)], 0).T[:S]
    angles = code_cols * (2.0 * jnp.pi / 256.0)
    cosines, sines = jnp.cos(angles), jnp.sin(angles)
    for place in range(N_TILE):
        cos_ref[place] = jnp.broadcast_to(cosines[:, place : place + 1], (S, BR))
        sin_ref[place] = jnp.broadcast_to(sines[:, place : place + 1], (S, BR))


def planned(*mains):
    vmem = pl.BlockSpec(memory_space=pltpu.VMEM)
    turn = jax.ShapeDtypeStruct((N_TILE, S, BR), jnp.float32)
    return pl.pallas_call(
        plan_kernel,
        out_shape=[jax.ShapeDtypeStruct((8, WIN), jnp.int32), turn, turn],
        in_specs=[vmem] * SIDE,
        out_specs=[vmem] * 3,
        compiler_params=pltpu.CompilerParams(vmem_limit_bytes=8 * 2**20),
        name="planned",
    )(*(pltpu.with_memory_space_constraint(v, pltpu.VMEM) for v in mains))


def interleave(real, imag):
    pieces = []
    for d in range(N_LINE):
        pieces += [real[8 * d : 8 * d + 8], imag[8 * d : 8 * d + 8]]
    return jnp.concatenate(pieces, 0)


def image_kernel(plan_ref, *refs):
    main_refs = refs[:SIDE]
    rim_ref, cos_ref, sin_ref, table_ref, matrix_ref, _, out_ref, held_ref = refs[SIDE : SIDE + 8]
    slots_re, slots_im, total, sems = refs[SIDE + 8 :]
    copies = piece_copies(2, matrix_ref, held_ref, sems)
    for copy in copies:
        copy.start()
    count = plan_ref[1, SIDE]

    def make_slot(group, n):
        entry = plan_ref[0, jnp.minimum(n, MAXB - 1)]
        place, f, b = (entry >> 8) & 15, (entry >> 4) & 15, entry & 15
        w, i, main_ref = b >> 1, place & 3, main_refs[group]
        head = main_ref[i, pl.ds(pl.multiple_of(w * HALF, HALF), HALF), :]
        tail = main_ref[i, pl.ds(pl.multiple_of(jnp.minimum(w + 1, 7) * HALF, HALF), HALF), :]
        window = jnp.concatenate([head, jnp.where(w == 7, rim_ref[i, group], tail)], 0)
        stacked = lax.dot_general(
            window, table_ref[2 * f + (b & 1)], (((0,), (0,)), ((), ())), preferred_element_type=jnp.float32
        )
        real = stacked[:S, :BR] - stacked[S:, BR:]
        imag = stacked[S:, :BR] + stacked[:S, BR:]
        cosine, sine = cos_ref[SIDE * group + i], sin_ref[SIDE * group + i]
        turned_re = real * cosine + imag * sine
        turned_im = imag * cosine - real * sine
        return interleave(turned_re, turned_im).astype(jnp.bfloat16), interleave(-turned_im, turned_re).astype(jnp.bfloat16)

    for group in range(SIDE):
        start, end = plan_ref[1, group], plan_ref[1, group + 1]

        def make_quad(c, carry, group=group, start=start):
            made = [make_slot(group, start + QUAD * c + k) for k in range(QUAD)]
            for k in range(QUAD):
                slots_re[start + QUAD * c + k], slots_im[start + QUAD * c + k] = made[k]
            return carry

        lax.fori_loop(0, (end - start + QUAD - 1) >> 2, make_quad, 0)
    for k in range(QUAD):
        slots_re[count + k] = jnp.zeros((2 * S, BR), jnp.bfloat16)
        slots_im[count + k] = jnp.zeros((2 * S, BR), jnp.bfloat16)
    total[...] = jnp.zeros_like(total)
    for copy in copies:
        copy.wait()

    def multiply(c, carry):
        at = []
        for k in range(QUAD):
            slot = plan_ref[0, jnp.minimum(QUAD * c + k, count - 1)] >> 12
            at.append(pl.ds(pl.multiple_of(slot * BR, BR), BR))
        matrix = jnp.concatenate([held_ref[part, rows, :] for part in range(2) for rows in at], 0)
        beams = [ref[QUAD * c + k] for ref in (slots_re, slots_im) for k in range(QUAD)]
        total[...] += jnp.dot(jnp.concatenate(beams, 1), matrix, preferred_element_type=jnp.float32)
        return carry

    lax.fori_loop(0, (count + QUAD - 1) >> 2, multiply, 0)
    for d in range(N_LINE):
        for depth in range(TZ):
            out_ref[d, depth] = total[16 * d : 16 * d + 16, TX * depth : TX * depth + TX].astype(jnp.bfloat16)


def partial_image(plan, mains, rims, turns, tables, beam_matrix, held):
    smem, vmem = pl.BlockSpec(memory_space=pltpu.SMEM), pl.BlockSpec(memory_space=pltpu.VMEM)
    fixed = [pltpu.with_memory_space_constraint(v, pltpu.VMEM) for v in (*mains, rims, *turns, tables)]
    fixed.append(pltpu.with_memory_space_constraint(beam_matrix, pltpu.HBM))
    room = MAXB + QUAD * 2
    return pl.pallas_call(
        image_kernel,
        out_shape=[
            pltpu.VMEM((N_LINE, TZ, 16, TX), jnp.bfloat16),
            pltpu.VMEM((2, MAXB * BR, WIDE), jnp.bfloat16),
        ],
        in_specs=[smem] + [vmem] * (len(fixed) - 1) + [pl.BlockSpec(memory_space=pltpu.HBM), vmem],
        out_specs=[vmem] * 2,
        scratch_shapes=[
            pltpu.VMEM((room, 2 * S, BR), jnp.bfloat16),
            pltpu.VMEM((room, 2 * S, BR), jnp.bfloat16),
            pltpu.VMEM((2 * S, WIDE), jnp.float32),
            pltpu.SemaphoreType.DMA((2 * STREAMS,)),
        ],
        input_output_aliases={1 + len(fixed): 1},
        compiler_params=pltpu.CompilerParams(vmem_limit_bytes=6 * 2**20),
        name="partial_image",
    )(plan, *fixed, pltpu.with_memory_space_constraint(held, pltpu.VMEM))[0]


def sum_kernel(parts_ref, out_ref, first_ref, second_ref):
    odd = (lax.axis_index("tile") & 1) == 1
    totals = []
    for depth in range(TZ):
        total = parts_ref[0, depth].astype(jnp.float32)
        for line in range(1, N_LINE):
            total = total + parts_ref[line, depth].astype(jnp.float32)
        out_ref[depth] = total
        totals.append(total)
    for row in range(2):
        top, bottom = totals[row], totals[TZ - 2 + row]
        first_ref[row] = jnp.where(odd, top, bottom)
        second_ref[row] = jnp.where(odd, bottom, top)


def summed_lines(parts):
    shapes = [jax.ShapeDtypeStruct((rows, 16, TX), jnp.float32) for rows in (TZ, 2, 2)]
    return pl.pallas_call(
        sum_kernel,
        out_shape=shapes,
        in_specs=[pl.BlockSpec(memory_space=pltpu.VMEM)],
        out_specs=[pl.BlockSpec(memory_space=pltpu.VMEM)] * 3,
        compiler_params=pltpu.CompilerParams(vmem_limit_bytes=8 * 2**20),
        name="summed_lines",
    )(parts)


def add_filtered(filter_ref, results, sources):
    lane = lax.broadcasted_iota(jnp.int32, (16, TX), 1)
    for side in range(5):
        move = side - 2
        inside = (lane + move >= 0) & (lane + move < TX)
        for source, row in sources:
            if move:
                row = jnp.where(inside, pltpu.roll(row, (-move) % TX, 1), 0.0)
            for depth in range(max(0, source - 4), min(TZ, source + 1)):
                results[depth] = results[depth] + filter_ref[source - depth, side] * row
    return results


def inner_kernel(filter_ref, image_ref, out_ref):
    results = [jnp.zeros((16, TX), jnp.float32) for _ in range(TZ)]
    results = add_filtered(filter_ref, results, [(depth + 2, image_ref[depth]) for depth in range(TZ)])
    for depth in range(TZ):
        out_ref[depth] = results[depth]


def outer_kernel(filter_ref, first_ref, inner_ref, second_ref, out_ref):
    odd = (lax.axis_index("tile") & 1) == 1
    sources = [(row, jnp.where(odd, first_ref[row], second_ref[row])) for row in range(2)]
    sources += [(TZ + 2 + row, jnp.where(odd, second_ref[row], first_ref[row])) for row in range(2)]
    results = add_filtered(filter_ref, [inner_ref[depth] for depth in range(TZ)], sources)
    for depth in range(TZ):
        for part in range(2):
            out_ref[pl.ds(part * 64 + depth, 8, stride=TZ), :] = results[depth][8 * part : 8 * part + 8]


def dip_call(kernel, shape, dip_filter, *arrays):
    vmem = pl.BlockSpec(memory_space=pltpu.VMEM)
    return pl.pallas_call(
        kernel,
        out_shape=jax.ShapeDtypeStruct(shape, jnp.float32),
        in_specs=[pl.BlockSpec(memory_space=pltpu.SMEM)] + [vmem] * len(arrays),
        out_specs=vmem,
        compiler_params=pltpu.CompilerParams(vmem_limit_bytes=2 * 2**20),
    )(dip_filter, *arrays)


def spread(value, x_first, offsets=RING[1:]):
    received = []
    for offset in offsets:
        received.append(lax.ppermute(value, BOTH, hops(offset, x_first)))
    return received


def per_device(traces, codes, routes, beam_matrix, dip_filter):
    main = first_rows(traces, routes, codes)
    near = jnp.stack([main] + spread(main, False))
    mains = [near] + spread(near, True)
    plan, *turns = planned(*mains)
    tables, held = slant_tables(beam_matrix)
    rim = lax.ppermute(near[:, :HALF], "line", [(i + 1, i) for i in range(N_LINE - 1)])
    rims = jnp.stack([rim] + spread(rim, False))
    held = held_more(beam_matrix, held)
    image = partial_image(plan, mains, rims, turns, tables, beam_matrix, held)
    parts = lax.all_to_all(image, "line", 0, 0, tiled=True)
    image, first, second = summed_lines(parts)
    inner = dip_call(inner_kernel, (TZ, 16, TX), dip_filter, image)
    first = lax.ppermute(first, "tile", [(i, i ^ 1) for i in range(N_TILE)])
    second = lax.ppermute(second, "tile", [(i, ((i - 1) ^ 1) + 1) for i in range(1, N_TILE - 1)])
    return dip_call(outer_kernel, (2 * 8 * TZ, TX), dip_filter, first, inner, second).reshape(2, 8, TZ, TX)


def solution(mesh):
    in_specs = (
        P("tile", "line", None),
        P("tile", None),
        P("line", "tile"),
        P("line", "tile", None, None, None),
        P(),
    )
    out_specs = P(None, "line", "tile", None)

    return jax.shard_map(per_device, mesh=mesh, in_specs=in_specs, out_specs=out_specs, check_vma=False)
```

```python
import jax
import jax.numpy as jnp
from jax import lax
from jax.experimental import pallas as pl
from jax.experimental.pallas import tpu as pltpu
from jax.sharding import PartitionSpec as P


S = 64
P_SIZE = 256
WIN = 128
BR = 128
TZ = 8
TX = 128
MAXB = 32
NB = 16
HALF = WIN // 2
LOCAL = 512
ROWS = LOCAL + 8
SIDE = 4
RING = (0, 1, 3, 2)
BOTH = ("line", "tile")
N_LINE = 8
N_TILE = 16
QUAD = 4
OCT = 8
PIECES = (0, 1408, 2432, MAXB * BR)
STREAMS = 4
WIDE = TZ * TX


def hops(offset, x_first):
    pairs = []
    for line in range(N_LINE):
        along_x = x_first == (line % 2 == 0)
        for x in range(SIDE):
            for z in range(SIDE):
                to_x, to_z = ((x + offset) % SIDE, z) if along_x else (x, (z + offset) % SIDE)
                pairs.append((line * N_TILE + x * SIDE + z, line * N_TILE + to_x * SIDE + to_z))
    return pairs


def first_kernel(traces_ref, routes_ref, codes_ref, main_ref, rows, routes_v, codes_v, sems):
    copies = (
        pltpu.make_async_copy(traces_ref.at[0], main_ref.at[pl.ds(0, LOCAL)], sems.at[0]),
        pltpu.make_async_copy(routes_ref, routes_v, sems.at[1]),
        pltpu.make_async_copy(codes_ref, codes_v, sems.at[2]),
    )
    for copy in copies:
        copy.start()
    rows[...] = jnp.zeros_like(rows)
    for copy in copies:
        copy.wait()
    rows[0:1, :NB] = routes_v[...].astype(jnp.float32)
    rows[1:2, :S] = codes_v[...].astype(jnp.float32)
    main_ref[LOCAL:] = rows[...].astype(jnp.bfloat16)


def first_rows(traces, routes, codes):
    return pl.pallas_call(
        first_kernel,
        out_shape=pltpu.VMEM((ROWS, WIN), jnp.bfloat16),
        in_specs=[pl.BlockSpec(memory_space=pltpu.HBM)] * 3,
        out_specs=pl.BlockSpec(memory_space=pltpu.VMEM),
        scratch_shapes=[
            pltpu.VMEM((8, WIN), jnp.float32),
            pltpu.VMEM((1, NB), jnp.int32),
            pltpu.VMEM((1, S), jnp.int32),
            pltpu.SemaphoreType.DMA((3,)),
        ],
        compiler_params=pltpu.CompilerParams(vmem_limit_bytes=2 * 2**20),
        name="first_rows",
    )(*(pltpu.with_memory_space_constraint(v, pltpu.HBM) for v in (traces, routes, codes)))


def table_kernel(matrix_ref, table_ref, held_ref, sems):
    copies = piece_copies(0, matrix_ref, held_ref, sems)
    for copy in copies:
        copy.start()
    rows = lax.broadcasted_iota(jnp.int32, (WIN, P_SIZE), 0)
    cols = lax.broadcasted_iota(jnp.int32, (WIN, P_SIZE), 1)
    turns = (cols - P_SIZE // 2) * (2 * rows - (WIN - 1))
    unit = 2.0 * jnp.pi / 8192.0
    step = (((turns + 4096) & 8191) - 4096).astype(jnp.float32) * unit
    base = (((32 * turns + 4096) & 8191) - 4096).astype(jnp.float32) * unit
    offsets = lax.broadcasted_iota(jnp.int32, (WIN, 1), 0).astype(jnp.float32) - (WIN - 1) / 2
    taper = jnp.exp(-0.5 * (offsets / (0.4 * WIN)) ** 2)
    taper = taper / jnp.sqrt(jnp.sum(taper * taper, axis=0, keepdims=True))
    step_c, step_s = jnp.cos(step), jnp.sin(step)
    now_c, now_s = taper * jnp.cos(base), -taper * jnp.sin(base)
    for f in range(N_TILE):
        for q in range(2):
            half = slice(q * BR, (q + 1) * BR)
            table_ref[2 * f + q, :, :BR] = now_c[:, half].astype(jnp.bfloat16)
            table_ref[2 * f + q, :, BR:] = now_s[:, half].astype(jnp.bfloat16)
        now_c, now_s = now_c * step_c + now_s * step_s, now_s * step_c - now_c * step_s
    for copy in copies:
        copy.wait()


def slant_tables(beam_matrix):
    vmem = pl.BlockSpec(memory_space=pltpu.VMEM)
    return pl.pallas_call(
        table_kernel,
        out_shape=[
            pltpu.VMEM((2 * N_TILE, WIN, 2 * BR), jnp.bfloat16),
            pltpu.VMEM((2, MAXB * BR, WIDE), jnp.bfloat16),
        ],
        in_specs=[pl.BlockSpec(memory_space=pltpu.HBM)],
        out_specs=[vmem] * 2,
        scratch_shapes=[pltpu.SemaphoreType.DMA((2 * STREAMS,))],
        compiler_params=pltpu.CompilerParams(vmem_limit_bytes=4 * 2**20),
        name="slant_tables",
    )(pltpu.with_memory_space_constraint(beam_matrix, pltpu.HBM))


def piece_copies(piece, matrix_ref, held_ref, sems):
    copies = []
    first, rows = PIECES[piece], (PIECES[piece + 1] - PIECES[piece]) // STREAMS
    for part in range(2):
        for k in range(STREAMS):
            at = pl.ds(first + k * rows, rows)
            source, target = matrix_ref.at[0, 0, part, at, :], held_ref.at[part, at, :]
            copies.append(pltpu.make_async_copy(source, target, sems.at[len(copies)]))
    return copies


def hold_kernel(matrix_ref, before_ref, held_ref, sems):
    copies = piece_copies(1, matrix_ref, held_ref, sems)
    for copy in copies:
        copy.start()
    for copy in copies:
        copy.wait()


def held_more(beam_matrix, held):
    hbm, vmem = pl.BlockSpec(memory_space=pltpu.HBM), pl.BlockSpec(memory_space=pltpu.VMEM)
    return pl.pallas_call(
        hold_kernel,
        out_shape=pltpu.VMEM((2, MAXB * BR, WIDE), jnp.bfloat16),
        in_specs=[hbm, vmem],
        out_specs=vmem,
        scratch_shapes=[pltpu.SemaphoreType.DMA((2 * STREAMS,))],
        input_output_aliases={1: 0},
        compiler_params=pltpu.CompilerParams(vmem_limit_bytes=2 * 2**20),
        name="held_more",
    )(pltpu.with_memory_space_constraint(beam_matrix, pltpu.HBM), pltpu.with_memory_space_constraint(held, pltpu.VMEM))


def offset_of(place):
    return jnp.where(place == 3, 2, jnp.where(place == 2, 3, place))


def write_plan(main_refs, plan_ref, cos_ref, sin_ref, plan_copy):
    tile = lax.axis_index("tile")
    x, z, parity = tile >> 2, tile & 3, lax.axis_index("line") & 1
    rows = [ref[i, LOCAL : LOCAL + 8, :].astype(jnp.float32) for ref in main_refs for i in range(SIDE)]
    routes, codes = (jnp.concatenate([row[k : k + 1] for row in rows], 0) for k in range(2))

    def sender(place):
        far, near = offset_of(place >> 2), offset_of(place & 3)
        dx, dz = jnp.where(parity == 0, far, near), jnp.where(parity == 0, near, far)
        return (((x - dx) & 3) << 2) + ((z - dz) & 3)

    wide = (N_TILE, WIN)
    place_r, lane = lax.broadcasted_iota(jnp.int32, wide, 0), lax.broadcasted_iota(jnp.int32, wide, 1)
    sender_r = sender(place_r)
    mine = jnp.where((lane < NB) & (routes == tile.astype(jnp.float32)), 1.0, 0.0)
    lane_r, lane_c = (lax.broadcasted_iota(jnp.int32, (WIN, WIN), axis) for axis in (0, 1))
    before_b = jnp.dot(mine, jnp.where(lane_r < lane_c, 1.0, 0.0), preferred_element_type=jnp.float32)
    counts = jnp.dot(mine, jnp.ones((WIN, WIN), jnp.float32), preferred_element_type=jnp.float32)
    place_a, place_b = (lax.broadcasted_iota(jnp.int32, (N_TILE, N_TILE), axis) for axis in (0, 1))
    earlier = jnp.where(sender(place_b) < sender(place_a), 1.0, 0.0)
    before_sender = jnp.dot(earlier, counts, preferred_element_type=jnp.float32)
    before_place = jnp.dot(jnp.where(place_b < place_a, 1.0, 0.0), counts, preferred_element_type=jnp.float32)
    slot, spot = before_sender + before_b, before_place + before_b
    spot = jnp.where(mine > 0.0, spot, -1.0)
    entry = slot * 4096.0 + (place_r * 256 + sender_r * NB + lane).astype(jnp.float32)
    lane_f = lane.astype(jnp.float32)
    entries = jnp.zeros(wide, jnp.float32)
    for b in range(NB):
        entries = entries + jnp.where(spot[:, b : b + 1] == lane_f, entry[:, b : b + 1], 0.0)
    starts = jnp.where(place_r == SIDE * lane, before_place, 0.0) + jnp.where(lane == SIDE, counts, 0.0)
    starts = jnp.sum(starts, 0, keepdims=True)
    entries = jnp.sum(entries, 0, keepdims=True)
    plan_ref[...] = jnp.concatenate([entries, starts, jnp.zeros((6, WIN), jnp.float32)], 0).astype(jnp.int32)

    plan_copy.start()
    code_cols = jnp.concatenate([codes, jnp.zeros((WIN - N_TILE, WIN), jnp.float32)], 0).T[:S]
    angles = code_cols * (2.0 * jnp.pi / 256.0)
    cosines, sines = jnp.cos(angles), jnp.sin(angles)
    for place in range(N_TILE):
        cos_ref[place] = jnp.broadcast_to(cosines[:, place : place + 1], (S, BR))
        sin_ref[place] = jnp.broadcast_to(sines[:, place : place + 1], (S, BR))
    plan_copy.wait()


def interleave(real, imag):
    pieces = []
    for d in range(N_LINE):
        pieces += [real[8 * d : 8 * d + 8], imag[8 * d : 8 * d + 8]]
    return jnp.concatenate(pieces, 0)


def image_kernel(*refs):
    main_refs = refs[:SIDE]
    rim_ref, table_ref, matrix_ref, _, out_ref, held_ref = refs[SIDE : SIDE + 6]
    slots_re, slots_im, total, plan_v, plan_ref, cos_ref, sin_ref, plan_sem, sems = refs[SIDE + 6 :]
    copies = piece_copies(2, matrix_ref, held_ref, sems)
    for copy in copies:
        copy.start()
    write_plan(main_refs, plan_v, cos_ref, sin_ref, pltpu.make_async_copy(plan_v, plan_ref, plan_sem))
    count = plan_ref[1, SIDE]

    def make_slot(group, n):
        entry = plan_ref[0, jnp.minimum(n, MAXB - 1)]
        place, f, b = (entry >> 8) & 15, (entry >> 4) & 15, entry & 15
        w, i, main_ref = b >> 1, place & 3, main_refs[group]
        head = main_ref[i, pl.ds(pl.multiple_of(w * HALF, HALF), HALF), :]
        tail = main_ref[i, pl.ds(pl.multiple_of(jnp.minimum(w + 1, 7) * HALF, HALF), HALF), :]
        window = jnp.concatenate([head, jnp.where(w == 7, rim_ref[i, group], tail)], 0)
        stacked = lax.dot_general(
            window, table_ref[2 * f + (b & 1)], (((0,), (0,)), ((), ())), preferred_element_type=jnp.float32
        )
        real = stacked[:S, :BR] - stacked[S:, BR:]
        imag = stacked[S:, :BR] + stacked[:S, BR:]
        cosine, sine = cos_ref[SIDE * group + i], sin_ref[SIDE * group + i]
        turned_re = real * cosine + imag * sine
        turned_im = imag * cosine - real * sine
        return interleave(turned_re, turned_im).astype(jnp.bfloat16), interleave(-turned_im, turned_re).astype(jnp.bfloat16)

    for group in range(SIDE):
        start, end = plan_ref[1, group], plan_ref[1, group + 1]

        def make_quad(c, carry, group=group, start=start):
            made = [make_slot(group, start + QUAD * c + k) for k in range(QUAD)]
            for k in range(QUAD):
                slots_re[start + QUAD * c + k], slots_im[start + QUAD * c + k] = made[k]
            return carry

        lax.fori_loop(0, (end - start + QUAD - 1) >> 2, make_quad, 0)

    @pl.when((count & (OCT - 1)) != 0)
    def _():
        for k in range(OCT):
            slots_re[count + k] = jnp.zeros((2 * S, BR), jnp.bfloat16)
            slots_im[count + k] = jnp.zeros((2 * S, BR), jnp.bfloat16)

    total[...] = jnp.zeros_like(total)
    for copy in copies:
        copy.wait()

    def multiply(c, carry):
        at = []
        for k in range(OCT):
            slot = plan_ref[0, jnp.minimum(OCT * c + k, count - 1)] >> 12
            at.append(pl.ds(pl.multiple_of(slot * BR, BR), BR))
        matrix = jnp.concatenate([held_ref[part, rows, :] for part in range(2) for rows in at], 0)
        beams = [ref[OCT * c + k] for ref in (slots_re, slots_im) for k in range(OCT)]
        total[...] += jnp.dot(jnp.concatenate(beams, 1), matrix, preferred_element_type=jnp.float32)
        return carry

    lax.fori_loop(0, (count + OCT - 1) >> 3, multiply, 0)
    for d in range(N_LINE):
        for depth in range(TZ):
            out_ref[d, depth] = total[16 * d : 16 * d + 16, TX * depth : TX * depth + TX].astype(jnp.bfloat16)


def partial_image(mains, rims, tables, beam_matrix, held):
    vmem = pl.BlockSpec(memory_space=pltpu.VMEM)
    fixed = [pltpu.with_memory_space_constraint(v, pltpu.VMEM) for v in (*mains, rims, tables)]
    fixed.append(pltpu.with_memory_space_constraint(beam_matrix, pltpu.HBM))
    room = MAXB + OCT
    return pl.pallas_call(
        image_kernel,
        out_shape=[
            pltpu.VMEM((N_LINE, TZ, 16, TX), jnp.bfloat16),
            pltpu.VMEM((2, MAXB * BR, WIDE), jnp.bfloat16),
        ],
        in_specs=[vmem] * (len(fixed) - 1) + [pl.BlockSpec(memory_space=pltpu.HBM), vmem],
        out_specs=[vmem] * 2,
        scratch_shapes=[
            pltpu.VMEM((room, 2 * S, BR), jnp.bfloat16),
            pltpu.VMEM((room, 2 * S, BR), jnp.bfloat16),
            pltpu.VMEM((2 * S, WIDE), jnp.float32),
            pltpu.VMEM((8, WIN), jnp.int32),
            pltpu.SMEM((8, WIN), jnp.int32),
            pltpu.VMEM((N_TILE, S, BR), jnp.float32),
            pltpu.VMEM((N_TILE, S, BR), jnp.float32),
            pltpu.SemaphoreType.DMA,
            pltpu.SemaphoreType.DMA((2 * STREAMS,)),
        ],
        input_output_aliases={len(fixed): 1},
        compiler_params=pltpu.CompilerParams(vmem_limit_bytes=8 * 2**20),
        name="partial_image",
    )(*fixed, pltpu.with_memory_space_constraint(held, pltpu.VMEM))[0]


def sum_kernel(parts_ref, out_ref, first_ref, second_ref):
    odd = (lax.axis_index("tile") & 1) == 1
    totals = []
    for depth in range(TZ):
        total = parts_ref[0, depth].astype(jnp.float32)
        for line in range(1, N_LINE):
            total = total + parts_ref[line, depth].astype(jnp.float32)
        out_ref[depth] = total
        totals.append(total)
    for row in range(2):
        top, bottom = totals[row], totals[TZ - 2 + row]
        first_ref[row] = jnp.where(odd, top, bottom)
        second_ref[row] = jnp.where(odd, bottom, top)


def summed_lines(parts):
    shapes = [pltpu.VMEM((rows, 16, TX), jnp.float32) for rows in (TZ, 2, 2)]
    return pl.pallas_call(
        sum_kernel,
        out_shape=shapes,
        in_specs=[pl.BlockSpec(memory_space=pltpu.VMEM)],
        out_specs=[pl.BlockSpec(memory_space=pltpu.VMEM)] * 3,
        compiler_params=pltpu.CompilerParams(vmem_limit_bytes=8 * 2**20),
        name="summed_lines",
    )(pltpu.with_memory_space_constraint(parts, pltpu.VMEM))


def add_filtered(tap, results, sources):
    lane = lax.broadcasted_iota(jnp.int32, (16, TX), 1)
    for side in range(5):
        move = side - 2
        inside = (lane + move >= 0) & (lane + move < TX)
        for source, row in sources:
            if move:
                row = jnp.where(inside, pltpu.roll(row, (-move) % TX, 1), 0.0)
            for depth in range(max(0, source - 4), min(TZ, source + 1)):
                results[depth] = results[depth] + tap(source - depth, side) * row
    return results


def inner_kernel(filter_ref, image_ref, out_ref, taps_ref):
    results = [jnp.zeros((16, TX), jnp.float32) for _ in range(TZ)]
    sources = [(depth + 2, image_ref[depth]) for depth in range(TZ)]
    results = add_filtered(lambda down, side: filter_ref[down, side], results, sources)
    for depth in range(TZ):
        out_ref[depth] = results[depth]
    for down in range(5):
        for side in range(5):
            taps_ref[5 * down + side : 5 * down + side + 1] = jnp.full((1, TX), filter_ref[down, side], jnp.float32)


def outer_kernel(taps_ref, first_ref, inner_ref, second_ref, out_ref):
    odd = (lax.axis_index("tile") & 1) == 1
    sources = [(row, jnp.where(odd, first_ref[row], second_ref[row])) for row in range(2)]
    sources += [(TZ + 2 + row, jnp.where(odd, second_ref[row], first_ref[row])) for row in range(2)]
    results = add_filtered(
        lambda down, side: taps_ref[5 * down + side : 5 * down + side + 1],
        [inner_ref[depth] for depth in range(TZ)],
        sources,
    )
    for depth in range(TZ):
        for part in range(2):
            out_ref[pl.ds(part * 64 + depth, 8, stride=TZ), :] = results[depth][8 * part : 8 * part + 8]


def inner_filtered(dip_filter, image):
    vmem = pl.BlockSpec(memory_space=pltpu.VMEM)
    return pl.pallas_call(
        inner_kernel,
        out_shape=[pltpu.VMEM((TZ, 16, TX), jnp.float32), pltpu.VMEM((32, TX), jnp.float32)],
        in_specs=[pl.BlockSpec(memory_space=pltpu.SMEM), vmem],
        out_specs=[vmem] * 2,
        compiler_params=pltpu.CompilerParams(vmem_limit_bytes=2 * 2**20),
        name="inner_filtered",
    )(dip_filter, pltpu.with_memory_space_constraint(image, pltpu.VMEM))


def outer_filtered(*arrays):
    vmem = pl.BlockSpec(memory_space=pltpu.VMEM)
    return pl.pallas_call(
        outer_kernel,
        out_shape=jax.ShapeDtypeStruct((2 * 8 * TZ, TX), jnp.float32),
        in_specs=[vmem] * len(arrays),
        out_specs=vmem,
        compiler_params=pltpu.CompilerParams(vmem_limit_bytes=2 * 2**20),
        name="outer_filtered",
    )(*(pltpu.with_memory_space_constraint(v, pltpu.VMEM) for v in arrays))


def spread(value, x_first, offsets=RING[1:]):
    received = []
    for offset in offsets:
        received.append(lax.ppermute(value, BOTH, hops(offset, x_first)))
    return received


def per_device(traces, codes, routes, beam_matrix, dip_filter):
    main = first_rows(traces, routes, codes)
    near = jnp.stack([main] + spread(main, False))
    mains = [near] + spread(near, True)
    tables, held = slant_tables(beam_matrix)
    rim = lax.ppermute(near[:, :HALF], "line", [(i + 1, i) for i in range(N_LINE - 1)])
    rims = jnp.stack([rim] + spread(rim, False))
    held = held_more(beam_matrix, held)
    image = partial_image(mains, rims, tables, beam_matrix, held)
    parts = lax.all_to_all(image, "line", 0, 0, tiled=True)
    image, first, second = summed_lines(parts)
    inner, taps = inner_filtered(dip_filter, image)
    first = lax.ppermute(first, "tile", [(i, i ^ 1) for i in range(N_TILE)])
    second = lax.ppermute(second, "tile", [(i, ((i - 1) ^ 1) + 1) for i in range(1, N_TILE - 1)])
    return outer_filtered(taps, first, inner, second).reshape(2, 8, TZ, TX)


def solution(mesh):
    in_specs = (
        P("tile", "line", None),
        P("tile", None),
        P("line", "tile"),
        P("line", "tile", None, None, None),
        P(),
    )
    out_specs = P(None, "line", "tile", None)

    return jax.shard_map(per_device, mesh=mesh, in_specs=in_specs, out_specs=out_specs, check_vma=False)
```

```python
import jax
import jax.numpy as jnp
from jax import lax
from jax.experimental import pallas as pl
from jax.experimental.pallas import tpu as pltpu
from jax.sharding import PartitionSpec as P


S = 64
P_SIZE = 256
WIN = 128
BR = 128
TZ = 8
TX = 128
MAXB = 32
NB = 16
HALF = WIN // 2
LOCAL = 512
ROWS = LOCAL + 8
SIDE = 4
RING = (0, 1, 3, 2)
BOTH = ("line", "tile")
N_LINE = 8
N_TILE = 16
QUAD = 4
OCT = 8
PIECES = (0, 1152, 2176, MAXB * BR)
STREAMS = 4
WIDE = TZ * TX


def hops(offset, x_first):
    pairs = []
    for line in range(N_LINE):
        along_x = x_first == (line % 2 == 0)
        for x in range(SIDE):
            for z in range(SIDE):
                to_x, to_z = ((x + offset) % SIDE, z) if along_x else (x, (z + offset) % SIDE)
                pairs.append((line * N_TILE + x * SIDE + z, line * N_TILE + to_x * SIDE + to_z))
    return pairs


def first_kernel(traces_ref, routes_ref, codes_ref, main_ref, rows, routes_v, codes_v, sems):
    copies = (
        pltpu.make_async_copy(traces_ref.at[0], main_ref.at[pl.ds(0, LOCAL)], sems.at[0]),
        pltpu.make_async_copy(routes_ref, routes_v, sems.at[1]),
        pltpu.make_async_copy(codes_ref, codes_v, sems.at[2]),
    )
    for copy in copies:
        copy.start()
    rows[...] = jnp.zeros_like(rows)
    for copy in copies[1:]:
        copy.wait()
    rows[0:1, :NB] = routes_v[...].astype(jnp.float32)
    rows[1:2, :S] = codes_v[...].astype(jnp.float32)
    main_ref[LOCAL:] = rows[...].astype(jnp.bfloat16)
    copies[0].wait()


def first_rows(traces, routes, codes):
    return pl.pallas_call(
        first_kernel,
        out_shape=pltpu.VMEM((ROWS, WIN), jnp.bfloat16),
        in_specs=[pl.BlockSpec(memory_space=pltpu.HBM)] * 3,
        out_specs=pl.BlockSpec(memory_space=pltpu.VMEM),
        scratch_shapes=[
            pltpu.VMEM((8, WIN), jnp.float32),
            pltpu.VMEM((1, NB), jnp.int32),
            pltpu.VMEM((1, S), jnp.int32),
            pltpu.SemaphoreType.DMA((3,)),
        ],
        compiler_params=pltpu.CompilerParams(vmem_limit_bytes=2 * 2**20),
        name="first_rows",
    )(*(pltpu.with_memory_space_constraint(v, pltpu.HBM) for v in (traces, routes, codes)))


def table_kernel(matrix_ref, table_ref, held_ref, sems):
    copies = piece_copies(0, matrix_ref, held_ref, sems)
    for copy in copies:
        copy.start()
    rows = lax.broadcasted_iota(jnp.int32, (WIN, P_SIZE), 0)
    cols = lax.broadcasted_iota(jnp.int32, (WIN, P_SIZE), 1)
    turns = (cols - P_SIZE // 2) * (2 * rows - (WIN - 1))
    unit = 2.0 * jnp.pi / 8192.0
    step = (((turns + 4096) & 8191) - 4096).astype(jnp.float32) * unit
    base = (((32 * turns + 4096) & 8191) - 4096).astype(jnp.float32) * unit
    offsets = lax.broadcasted_iota(jnp.int32, (WIN, 1), 0).astype(jnp.float32) - (WIN - 1) / 2
    taper = jnp.exp(-0.5 * (offsets / (0.4 * WIN)) ** 2)
    taper = taper / jnp.sqrt(jnp.sum(taper * taper, axis=0, keepdims=True))
    step_c, step_s = jnp.cos(step), jnp.sin(step)
    now_c, now_s = taper * jnp.cos(base), -taper * jnp.sin(base)
    for f in range(N_TILE):
        for q in range(2):
            half = slice(q * BR, (q + 1) * BR)
            table_ref[2 * f + q, :, :BR] = now_c[:, half].astype(jnp.bfloat16)
            table_ref[2 * f + q, :, BR:] = now_s[:, half].astype(jnp.bfloat16)
        now_c, now_s = now_c * step_c + now_s * step_s, now_s * step_c - now_c * step_s
    for copy in copies:
        copy.wait()


def slant_tables(beam_matrix):
    vmem = pl.BlockSpec(memory_space=pltpu.VMEM)
    return pl.pallas_call(
        table_kernel,
        out_shape=[
            pltpu.VMEM((2 * N_TILE, WIN, 2 * BR), jnp.bfloat16),
            pltpu.VMEM((2, MAXB * BR, WIDE), jnp.bfloat16),
        ],
        in_specs=[pl.BlockSpec(memory_space=pltpu.HBM)],
        out_specs=[vmem] * 2,
        scratch_shapes=[pltpu.SemaphoreType.DMA((2 * STREAMS,))],
        compiler_params=pltpu.CompilerParams(vmem_limit_bytes=4 * 2**20),
        name="slant_tables",
    )(pltpu.with_memory_space_constraint(beam_matrix, pltpu.HBM))


def piece_copies(piece, matrix_ref, held_ref, sems):
    copies = []
    first, rows = PIECES[piece], (PIECES[piece + 1] - PIECES[piece]) // STREAMS
    for part in range(2):
        for k in range(STREAMS):
            at = pl.ds(first + k * rows, rows)
            source, target = matrix_ref.at[0, 0, part, at, :], held_ref.at[part, at, :]
            copies.append(pltpu.make_async_copy(source, target, sems.at[len(copies)]))
    return copies


def hold_kernel(matrix_ref, before_ref, held_ref, sems):
    copies = piece_copies(1, matrix_ref, held_ref, sems)
    for copy in copies:
        copy.start()
    for copy in copies:
        copy.wait()


def held_more(beam_matrix, held):
    hbm, vmem = pl.BlockSpec(memory_space=pltpu.HBM), pl.BlockSpec(memory_space=pltpu.VMEM)
    return pl.pallas_call(
        hold_kernel,
        out_shape=pltpu.VMEM((2, MAXB * BR, WIDE), jnp.bfloat16),
        in_specs=[hbm, vmem],
        out_specs=vmem,
        scratch_shapes=[pltpu.SemaphoreType.DMA((2 * STREAMS,))],
        input_output_aliases={1: 0},
        compiler_params=pltpu.CompilerParams(vmem_limit_bytes=2 * 2**20),
        name="held_more",
    )(pltpu.with_memory_space_constraint(beam_matrix, pltpu.HBM), pltpu.with_memory_space_constraint(held, pltpu.VMEM))


def offset_of(place):
    return jnp.where(place == 3, 2, jnp.where(place == 2, 3, place))


def write_plan(main_refs, plan_ref, cos_ref, sin_ref, plan_copy):
    tile = lax.axis_index("tile")
    x, z, parity = tile >> 2, tile & 3, lax.axis_index("line") & 1
    rows = [ref[i, LOCAL : LOCAL + 8, :].astype(jnp.float32) for ref in main_refs for i in range(SIDE)]
    routes, codes = (jnp.concatenate([row[k : k + 1] for row in rows], 0) for k in range(2))

    def sender(place):
        far, near = offset_of(place >> 2), offset_of(place & 3)
        dx, dz = jnp.where(parity == 0, far, near), jnp.where(parity == 0, near, far)
        return (((x - dx) & 3) << 2) + ((z - dz) & 3)

    wide = (N_TILE, WIN)
    place_r, lane = lax.broadcasted_iota(jnp.int32, wide, 0), lax.broadcasted_iota(jnp.int32, wide, 1)
    sender_r = sender(place_r)
    mine = jnp.where((lane < NB) & (routes == tile.astype(jnp.float32)), 1.0, 0.0)
    lane_r, lane_c = (lax.broadcasted_iota(jnp.int32, (WIN, WIN), axis) for axis in (0, 1))
    before_b = jnp.dot(mine, jnp.where(lane_r < lane_c, 1.0, 0.0), preferred_element_type=jnp.float32)
    counts = jnp.dot(mine, jnp.ones((WIN, WIN), jnp.float32), preferred_element_type=jnp.float32)
    place_a, place_b = (lax.broadcasted_iota(jnp.int32, (N_TILE, N_TILE), axis) for axis in (0, 1))
    earlier = jnp.where(sender(place_b) < sender(place_a), 1.0, 0.0)
    before_sender = jnp.dot(earlier, counts, preferred_element_type=jnp.float32)
    before_place = jnp.dot(jnp.where(place_b < place_a, 1.0, 0.0), counts, preferred_element_type=jnp.float32)
    slot, spot = before_sender + before_b, before_place + before_b
    spot = jnp.where(mine > 0.0, spot, -1.0)
    entry = slot * 4096.0 + (place_r * 256 + sender_r * NB + lane).astype(jnp.float32)
    lane_f = lane.astype(jnp.float32)
    entries = jnp.zeros(wide, jnp.float32)
    for b in range(NB):
        entries = entries + jnp.where(spot[:, b : b + 1] == lane_f, entry[:, b : b + 1], 0.0)
    starts = jnp.where(place_r == SIDE * lane, before_place, 0.0) + jnp.where(lane == SIDE, counts, 0.0)
    starts = jnp.sum(starts, 0, keepdims=True)
    entries = jnp.sum(entries, 0, keepdims=True)
    plan_ref[...] = jnp.concatenate([entries, starts, jnp.zeros((6, WIN), jnp.float32)], 0).astype(jnp.int32)

    plan_copy.start()
    code_cols = jnp.concatenate([codes, jnp.zeros((WIN - N_TILE, WIN), jnp.float32)], 0).T[:S]
    angles = code_cols * (2.0 * jnp.pi / 256.0)
    cosines, sines = jnp.cos(angles), jnp.sin(angles)
    for place in range(N_TILE):
        cos_ref[place] = jnp.broadcast_to(cosines[:, place : place + 1], (S, BR))
        sin_ref[place] = jnp.broadcast_to(sines[:, place : place + 1], (S, BR))
    plan_copy.wait()


def interleave(real, imag):
    pieces = []
    for d in range(N_LINE):
        pieces += [real[8 * d : 8 * d + 8], imag[8 * d : 8 * d + 8]]
    return jnp.concatenate(pieces, 0)


def image_kernel(*refs):
    main_refs = refs[:SIDE]
    rim_ref, table_ref, matrix_ref, _, out_ref, held_ref = refs[SIDE : SIDE + 6]
    slots_re, slots_im, total, plan_v, plan_ref, cos_ref, sin_ref, plan_sem, sems = refs[SIDE + 6 :]
    copies = piece_copies(2, matrix_ref, held_ref, sems)
    for copy in copies:
        copy.start()
    write_plan(main_refs, plan_v, cos_ref, sin_ref, pltpu.make_async_copy(plan_v, plan_ref, plan_sem))
    count = plan_ref[1, SIDE]

    def make_slot(group, n):
        entry = plan_ref[0, jnp.minimum(n, MAXB - 1)]
        place, f, b = (entry >> 8) & 15, (entry >> 4) & 15, entry & 15
        w, i, main_ref = b >> 1, place & 3, main_refs[group]
        head = main_ref[i, pl.ds(pl.multiple_of(w * HALF, HALF), HALF), :]
        tail = main_ref[i, pl.ds(pl.multiple_of(jnp.minimum(w + 1, 7) * HALF, HALF), HALF), :]
        window = jnp.concatenate([head, jnp.where(w == 7, rim_ref[i, group], tail)], 0)
        stacked = lax.dot_general(
            window, table_ref[2 * f + (b & 1)], (((0,), (0,)), ((), ())), preferred_element_type=jnp.float32
        )
        real = stacked[:S, :BR] - stacked[S:, BR:]
        imag = stacked[S:, :BR] + stacked[:S, BR:]
        cosine, sine = cos_ref[SIDE * group + i], sin_ref[SIDE * group + i]
        turned_re = real * cosine + imag * sine
        turned_im = imag * cosine - real * sine
        return interleave(turned_re, turned_im).astype(jnp.bfloat16), interleave(-turned_im, turned_re).astype(jnp.bfloat16)

    for group in range(SIDE):
        start, end = plan_ref[1, group], plan_ref[1, group + 1]

        def make_quad(c, carry, group=group, start=start):
            made = [make_slot(group, start + QUAD * c + k) for k in range(QUAD)]
            for k in range(QUAD):
                slots_re[start + QUAD * c + k], slots_im[start + QUAD * c + k] = made[k]
            return carry

        lax.fori_loop(0, (end - start + QUAD - 1) >> 2, make_quad, 0)

    @pl.when((count & (OCT - 1)) != 0)
    def _():
        for k in range(OCT):
            slots_re[count + k] = jnp.zeros((2 * S, BR), jnp.bfloat16)
            slots_im[count + k] = jnp.zeros((2 * S, BR), jnp.bfloat16)

    total[...] = jnp.zeros_like(total)
    for copy in copies:
        copy.wait()

    def multiply(c, carry):
        at = []
        for k in range(OCT):
            slot = plan_ref[0, jnp.minimum(OCT * c + k, count - 1)] >> 12
            at.append(pl.ds(pl.multiple_of(slot * BR, BR), BR))
        matrix = jnp.concatenate([held_ref[part, rows, :] for part in range(2) for rows in at], 0)
        beams = [ref[OCT * c + k] for ref in (slots_re, slots_im) for k in range(OCT)]
        total[...] += jnp.dot(jnp.concatenate(beams, 1), matrix, preferred_element_type=jnp.float32)
        return carry

    lax.fori_loop(0, (count + OCT - 1) >> 3, multiply, 0)
    for d in range(N_LINE):
        for depth in range(TZ):
            out_ref[d, depth] = total[16 * d : 16 * d + 16, TX * depth : TX * depth + TX].astype(jnp.bfloat16)


def partial_image(mains, rims, tables, beam_matrix, held):
    vmem = pl.BlockSpec(memory_space=pltpu.VMEM)
    fixed = [pltpu.with_memory_space_constraint(v, pltpu.VMEM) for v in (*mains, rims, tables)]
    fixed.append(pltpu.with_memory_space_constraint(beam_matrix, pltpu.HBM))
    room = MAXB + OCT
    return pl.pallas_call(
        image_kernel,
        out_shape=[
            pltpu.VMEM((N_LINE, TZ, 16, TX), jnp.bfloat16),
            pltpu.VMEM((2, MAXB * BR, WIDE), jnp.bfloat16),
        ],
        in_specs=[vmem] * (len(fixed) - 1) + [pl.BlockSpec(memory_space=pltpu.HBM), vmem],
        out_specs=[vmem] * 2,
        scratch_shapes=[
            pltpu.VMEM((room, 2 * S, BR), jnp.bfloat16),
            pltpu.VMEM((room, 2 * S, BR), jnp.bfloat16),
            pltpu.VMEM((2 * S, WIDE), jnp.float32),
            pltpu.VMEM((8, WIN), jnp.int32),
            pltpu.SMEM((8, WIN), jnp.int32),
            pltpu.VMEM((N_TILE, S, BR), jnp.float32),
            pltpu.VMEM((N_TILE, S, BR), jnp.float32),
            pltpu.SemaphoreType.DMA,
            pltpu.SemaphoreType.DMA((2 * STREAMS,)),
        ],
        input_output_aliases={len(fixed): 1},
        compiler_params=pltpu.CompilerParams(vmem_limit_bytes=8 * 2**20),
        name="partial_image",
    )(*fixed, pltpu.with_memory_space_constraint(held, pltpu.VMEM))[0]


def sum_kernel(parts_ref, out_ref, first_ref, second_ref):
    odd = (lax.axis_index("tile") & 1) == 1
    totals = []
    for depth in range(TZ):
        total = parts_ref[0, depth].astype(jnp.float32)
        for line in range(1, N_LINE):
            total = total + parts_ref[line, depth].astype(jnp.float32)
        out_ref[depth] = total
        totals.append(total)
    for row in range(2):
        top, bottom = totals[row], totals[TZ - 2 + row]
        first_ref[row] = jnp.where(odd, top, bottom)
        second_ref[row] = jnp.where(odd, bottom, top)


def summed_lines(parts):
    shapes = [pltpu.VMEM((rows, 16, TX), jnp.float32) for rows in (TZ, 2, 2)]
    return pl.pallas_call(
        sum_kernel,
        out_shape=shapes,
        in_specs=[pl.BlockSpec(memory_space=pltpu.VMEM)],
        out_specs=[pl.BlockSpec(memory_space=pltpu.VMEM)] * 3,
        compiler_params=pltpu.CompilerParams(vmem_limit_bytes=8 * 2**20),
        name="summed_lines",
    )(pltpu.with_memory_space_constraint(parts, pltpu.VMEM))


def add_filtered(tap, results, sources):
    lane = lax.broadcasted_iota(jnp.int32, (16, TX), 1)
    for side in range(5):
        move = side - 2
        inside = (lane + move >= 0) & (lane + move < TX)
        for source, row in sources:
            if move:
                row = jnp.where(inside, pltpu.roll(row, (-move) % TX, 1), 0.0)
            for depth in range(max(0, source - 4), min(TZ, source + 1)):
                results[depth] = results[depth] + tap(source - depth, side) * row
    return results


def inner_kernel(filter_ref, image_ref, out_ref, taps_ref):
    results = [jnp.zeros((16, TX), jnp.float32) for _ in range(TZ)]
    sources = [(depth + 2, image_ref[depth]) for depth in range(TZ)]
    results = add_filtered(lambda down, side: filter_ref[down, side], results, sources)
    for depth in range(TZ):
        out_ref[depth] = results[depth]
    for down in range(5):
        for side in range(5):
            taps_ref[5 * down + side : 5 * down + side + 1] = jnp.full((1, TX), filter_ref[down, side], jnp.float32)


def outer_kernel(taps_ref, first_ref, inner_ref, second_ref, out_ref):
    odd = (lax.axis_index("tile") & 1) == 1
    sources = [(row, jnp.where(odd, first_ref[row], second_ref[row])) for row in range(2)]
    sources += [(TZ + 2 + row, jnp.where(odd, second_ref[row], first_ref[row])) for row in range(2)]
    results = add_filtered(
        lambda down, side: taps_ref[5 * down + side : 5 * down + side + 1],
        [inner_ref[depth] for depth in range(TZ)],
        sources,
    )
    for depth in range(TZ):
        for part in range(2):
            out_ref[pl.ds(part * 64 + depth, 8, stride=TZ), :] = results[depth][8 * part : 8 * part + 8]


def inner_filtered(dip_filter, image):
    vmem = pl.BlockSpec(memory_space=pltpu.VMEM)
    return pl.pallas_call(
        inner_kernel,
        out_shape=[pltpu.VMEM((TZ, 16, TX), jnp.float32), pltpu.VMEM((32, TX), jnp.float32)],
        in_specs=[pl.BlockSpec(memory_space=pltpu.SMEM), vmem],
        out_specs=[vmem] * 2,
        compiler_params=pltpu.CompilerParams(vmem_limit_bytes=2 * 2**20),
        name="inner_filtered",
    )(dip_filter, pltpu.with_memory_space_constraint(image, pltpu.VMEM))


def outer_filtered(*arrays):
    vmem = pl.BlockSpec(memory_space=pltpu.VMEM)
    return pl.pallas_call(
        outer_kernel,
        out_shape=jax.ShapeDtypeStruct((2 * 8 * TZ, TX), jnp.float32),
        in_specs=[vmem] * len(arrays),
        out_specs=vmem,
        compiler_params=pltpu.CompilerParams(vmem_limit_bytes=2 * 2**20),
        name="outer_filtered",
    )(*(pltpu.with_memory_space_constraint(v, pltpu.VMEM) for v in arrays))


def spread(value, x_first, offsets=RING[1:]):
    received = []
    for offset in offsets:
        received.append(lax.ppermute(value, BOTH, hops(offset, x_first)))
    return received


def per_device(traces, codes, routes, beam_matrix, dip_filter):
    main = first_rows(traces, routes, codes)
    near = jnp.stack([main] + spread(main, False))
    mains = [near] + spread(near, True)
    tables, held = slant_tables(beam_matrix)
    rim = lax.ppermute(near[:, :HALF], "line", [(i + 1, i) for i in range(N_LINE - 1)])
    rims = jnp.stack([rim] + spread(rim, False))
    held = held_more(beam_matrix, held)
    image = partial_image(mains, rims, tables, beam_matrix, held)
    parts = lax.all_to_all(image, "line", 0, 0, tiled=True)
    image, first, second = summed_lines(parts)
    inner, taps = inner_filtered(dip_filter, image)
    first = lax.ppermute(first, "tile", [(i, i ^ 1) for i in range(N_TILE)])
    second = lax.ppermute(second, "tile", [(i, ((i - 1) ^ 1) + 1) for i in range(1, N_TILE - 1)])
    return outer_filtered(taps, first, inner, second).reshape(2, 8, TZ, TX)


def solution(mesh):
    in_specs = (
        P("tile", "line", None),
        P("tile", None),
        P("line", "tile"),
        P("line", "tile", None, None, None),
        P(),
    )
    out_specs = P(None, "line", "tile", None)

    return jax.shard_map(per_device, mesh=mesh, in_specs=in_specs, out_specs=out_specs, check_vma=False)
```
